768 devices in a mesh: group: 4 (over x), member: 8 (over z_hi, core), space: 24 (over z_lo, y).
Axes of the slice: x: 4, y: 8, z: 12 (z_hi: 4, z_lo: 3; z = z_hi * 3 + z_lo), core: 2. Of those that a mesh axis runs over, the one named last changes fastest.
Arguments:
- height_velocity_tensor: float32 [256, 3, 768, 128], P(('group', 'member'), None, 'space'), may hold values from -6 to 6
- obs_values: float32 [768, 192], P(('group', 'member', 'space')), may hold values from -6 to 6
- obs_precision: float32 [768, 192], P(('group', 'member', 'space')), may hold values from 0.3 to 3
- obs_index: int32 [768, 192], P(('group', 'member', 'space')), may hold values from 0 to 383, as said below
Outputs:
- analysis: float32 [256, 3, 768, 128], P(('group', 'member'), None, 'space')
The draws below stay inside these ranges and needn't reach their ends.
Inputs may be any that keep to these rules, and one draw needn't show every extreme that they name: `obs_index`: each row holds 192 distinct positions among the 384 values of its block.
All inputs are finite; a program needn't handle non-finite values.
Results may differ from the reference program's by a relative error of at most 0.00013.
Values sent between devices are 32-bit elements; how exact they have to be, the bound alone decides.
A program may use at most 32 MiB of HBM per device.

```python
import math
import jax
import jax.numpy as jnp
from jax import lax

TRAJECTORY_COUNT = 256
CX = 32
NY = 128
STEPS = 2
NX = 768
TILE_POINTS = 128
OBS_BLK = 192
BLOCKS = 768
N_GROUP = 4
N_MEMBER = 8
N_SPACE = 24


def draw_obs_index(key, part):
    keys = jax.random.split(jax.random.fold_in(key, 17), BLOCKS)

    def one_row(row_key):
        shuffled = jax.random.permutation(row_key, 3 * TILE_POINTS - 2) + 1
        picked = shuffled[:OBS_BLK - 2].astype(jnp.int32)
        first = jnp.zeros((1,), jnp.int32)
        last = jnp.full((1,), 3 * TILE_POINTS - 1, jnp.int32)
        return jnp.concatenate([first, last, picked])
    return jax.vmap(one_row)(keys)


def levels(own_key, dims, shards, least, top_value):
    gain = 1.0
    for axis_at, parts in shards:
        draws = jax.random.uniform(jax.random.fold_in(jax.random.fold_in(own_key, 6), axis_at), (parts,), jnp.float32, least / len(shards), top_value / len(shards))
        gain = gain * jnp.repeat(jnp.exp(draws), dims[axis_at] // parts).reshape((-1,) + (1,) * (len(dims) - 1 - axis_at))
    return gain


def scatter_about(stream_key, dims, scale, reach, cuts=(), kind=jnp.bfloat16):
    entries = jax.random.normal(stream_key, dims, jnp.float32) * scale
    if len(cuts) > 0:
        entries = levels(stream_key, dims, cuts, -0.22, 0.18) * entries
    return jnp.clip(entries, min=-reach, max=reach).astype(kind)


def setup_inputs(seed: int = 0) -> dict:
    streams_of = jax.random.split(jax.random.key(seed), 5)
    height_velocity_tensor = scatter_about(streams_of[0], (TRAJECTORY_COUNT, 3, NX, NY), 1.0, 6.0, ((0, 32), (2, 24)), jnp.float32)
    obs_values = scatter_about(streams_of[1], (BLOCKS, OBS_BLK), 1.0, 6.0, ((0, 768),), jnp.float32)
    obs_precision = jnp.clip(jnp.exp(math.log(3.0) - 2.3025851 * jax.random.uniform(streams_of[2], (BLOCKS, OBS_BLK), jnp.float32) ** levels(streams_of[2], (BLOCKS, OBS_BLK), ((0, 768),), -0.2, 0.2)), 0.3, 3.0)
    obs_index = draw_obs_index(jax.random.fold_in(streams_of[4], 71), 0)
    return {"height_velocity_tensor": height_velocity_tensor, "obs_values": obs_values, "obs_precision": obs_precision, "obs_index": obs_index}


grav_coef = 0.4
depth_coef = 0.4

def across_y(field):
    return jnp.roll(field, -1, axis=-1) - jnp.roll(field, 1, axis=-1)

def across_x(field):
    padded = jnp.pad(field, ((1, 1), (0, 0)))
    return padded[2:] - padded[:-2]

def trajectory_prediction(layered_quantities):
    height, flow_x, flow_y = (layered_quantities[0], layered_quantities[1], layered_quantities[2])
    for stepped in range(STEPS):
        new_x = flow_x - grav_coef * across_x(height)
        new_y = flow_y - grav_coef * across_y(height)
        height = height - depth_coef * (across_x(new_x) + across_y(new_y))
        flow_x, flow_y = (new_x, new_y)
    return jnp.stack([height, flow_x, flow_y])

def take_values(values, picks):
    return jnp.take(values, picks, axis=-1)

def make_transform(gram, pull):
    identity = jnp.eye(gram.shape[0], dtype=jnp.float32)
    factor = jnp.linalg.cholesky(identity + gram)
    inverse = jax.scipy.linalg.solve_triangular(factor, identity, lower=True)
    inner = jnp.dot(inverse, pull, precision=lax.Precision.HIGHEST)
    weights_mean = jnp.dot(inverse.T, inner, precision=lax.Precision.HIGHEST)
    return inverse + weights_mean[None, :]

def reference(height_velocity_tensor, obs_values, obs_precision, obs_index):
    predicted_model_vector = lax.map(trajectory_prediction, height_velocity_tensor)
    trajectory_clusters = N_GROUP * N_MEMBER
    tile_partition = predicted_model_vector.reshape(TRAJECTORY_COUNT, 3, N_SPACE, trajectory_clusters, TILE_POINTS)
    ens_mean = lax.optimization_barrier(jnp.mean(tile_partition, axis=0))
    anomaly = tile_partition - ens_mean
    anomaly_blocks = jnp.transpose(anomaly, (3, 2, 0, 1, 4)).reshape(trajectory_clusters, N_SPACE, TRAJECTORY_COUNT, 3 * TILE_POINTS)
    mean_blocks = jnp.transpose(ens_mean, (2, 1, 0, 3)).reshape(trajectory_clusters, N_SPACE, 3 * TILE_POINTS)
    picks = obs_index.reshape(trajectory_clusters, N_SPACE, OBS_BLK)
    seen = jax.vmap(jax.vmap(take_values))(anomaly_blocks, picks)
    seen_mean = jax.vmap(jax.vmap(take_values))(mean_blocks, picks)
    precision = obs_precision.reshape(trajectory_clusters, N_SPACE, OBS_BLK)
    observed = obs_values.reshape(trajectory_clusters, N_SPACE, OBS_BLK)
    scale = 1.0 / math.sqrt(TRAJECTORY_COUNT - 1)
    scaled = seen * precision[:, :, None, :] * scale
    innovation = precision * (observed - seen_mean) * scale
    columns = jnp.transpose(scaled, (2, 0, 1, 3)).reshape(TRAJECTORY_COUNT, -1)
    gram = jnp.dot(columns, columns.T, precision=lax.Precision.HIGHEST)
    pull = jnp.dot(columns, innovation.reshape(-1), precision=lax.Precision.HIGHEST)
    transform = make_transform(gram, pull)
    update = jnp.dot(transform, anomaly.reshape(TRAJECTORY_COUNT, -1), precision=lax.Precision.HIGHEST)
    result = ens_mean.reshape(1, -1) + update
    return result.reshape(TRAJECTORY_COUNT, 3, N_SPACE * CX, NY)
```

```python
import math

import jax
import jax.numpy as jnp
from jax import lax
from jax.experimental import pallas as pl
from jax.experimental.pallas import tpu as pltpu
from jax.sharding import PartitionSpec as P

GRAV = 0.4
DEPTH = 0.4
GROUPS, MEMBERS, SPACES = 4, 8, 24
NZ, NY_CHIPS = 12, 8
OWNERS = GROUPS * MEMBERS
ROWS = 32
LOCAL = 8
ENSEMBLE = OWNERS * LOCAL
FIELDS = 3
COLS = 128
CELLS = FIELDS * COLS
OBS = 192
HALO = 4
MESH = pl.DeviceIdType.MESH
F32 = jnp.float32
HIGHEST = lax.Precision.HIGHEST
SCALE = 1.0 / math.sqrt(ENSEMBLE - 1)


def dot_nt(a, b):
    return lax.dot_general(
        a, b, (((1,), (1,)), ((), ())), precision=HIGHEST, preferred_element_type=F32
    )


def dot_nn(a, b):
    return lax.dot_general(
        a, b, (((1,), (0,)), ((), ())), precision=HIGHEST, preferred_element_type=F32
    )


def place():
    group = lax.axis_index("group")
    member = lax.axis_index("member")
    space = lax.axis_index("space")
    return group, member, space


def owner_id(k):
    return {"group": k // MEMBERS, "member": lax.rem(k, MEMBERS)}


def z_id(z, core, y):
    return {"member": z // 3 * 2 + core, "space": lax.rem(z, 3) * NY_CHIPS + y}


def across_y(field):
    return pltpu.roll(field, COLS - 1, 1) - pltpu.roll(field, 1, 1)


class Forecast:
    def __init__(self, load, outside):
        self.load = load
        self.outside = outside
        self.known = {}

    def masked(self, row, value):
        flag = self.outside(row)
        return value if flag is None else jnp.where(flag, 0.0, value)

    def get(self, field, step, row):
        key = (field, step, row)
        if key not in self.known:
            self.known[key] = self.compute(field, step, row)
        return self.known[key]

    def compute(self, field, step, row):
        if step == 0:
            return self.masked(row, self.load(field, row))
        if field == 1:
            ahead, behind = self.get(0, step - 1, row + 1), self.get(0, step - 1, row - 1)
            return self.masked(row, self.get(1, step - 1, row) - GRAV * (ahead - behind))
        if field == 2:
            return self.get(2, step - 1, row) - GRAV * across_y(self.get(0, step - 1, row))
        ahead, behind = self.get(1, step, row + 1), self.get(1, step, row - 1)
        change = ahead - behind + across_y(self.get(2, step, row))
        return self.masked(row, self.get(0, step - 1, row) - DEPTH * change)


def gather_kernel(
    x_ref,
    x_halo_ref,
    obs_ref,
    index_ref,
    values_ref,
    gram_ref,
    halo,
    sendbuf,
    mine,
    corebuf,
    x_from,
    x_to,
    y_from,
    y_to,
    z_from,
    z_own,
    all_y,
    all_x,
    halo_send,
    halo_recv,
    a2a_send,
    a2a_recv,
    core_sem,
    x_sem,
    y_sem,
    z_sem,
    gy_sem,
    gx_sem,
    gc_sem,
):
    group, member, space = place()
    core = lax.rem(member, 2)
    z = member // 2 * 3 + space // NY_CHIPS
    y = lax.rem(space, NY_CHIPS)
    me = group * MEMBERS + member

    barrier = pltpu.get_barrier_semaphore()
    above, below = lax.rem(space + SPACES - 1, SPACES), lax.rem(space + 1, SPACES)
    peers = [{"space": above}, {"space": below}]
    peers += [owner_id(lax.rem(me + d, OWNERS)) for d in range(1, OWNERS)]
    y_peers = [
        {"space": space - y + lax.rem(y + d, NY_CHIPS)} for d in range(1, NY_CHIPS)
    ]
    z_peers = [z_id(lax.rem(z + d, NZ), core, y) for d in range(1, NZ)]
    peers += y_peers + z_peers
    for peer in peers:
        pl.semaphore_signal(barrier, inc=1, device_id=peer, device_id_type=MESH)

    cells = lax.broadcasted_iota(jnp.int32, (CELLS, OBS), 0)
    picked = jnp.where(cells == index_ref[0:1, :], 1.0, 0.0)
    spread = dot_nt(obs_ref[...], picked)
    weight = spread[1:2, :] * SCALE
    seen_value = spread[0:1, :]

    pl.semaphore_wait(barrier, len(peers))

    up = pltpu.make_async_remote_copy(
        src_ref=x_halo_ref.at[:, 0],
        dst_ref=halo.at[1],
        send_sem=halo_send.at[0],
        recv_sem=halo_recv.at[1],
        device_id={"space": above},
        device_id_type=MESH,
    )
    down = pltpu.make_async_remote_copy(
        src_ref=x_halo_ref.at[:, ROWS // HALO - 1],
        dst_ref=halo.at[0],
        send_sem=halo_send.at[1],
        recv_sem=halo_recv.at[0],
        device_id={"space": below},
        device_id_type=MESH,
    )
    up.start()
    down.start()

    flat = [halo.at[i].reshape(LOCAL * FIELDS * HALO, COLS) for i in range(2)]

    def load(field, row):
        if row < 0:
            start = field * HALO + row + HALO
            return flat[0][pl.ds(start, LOCAL, stride=FIELDS * HALO), :]
        if row >= ROWS:
            start = field * HALO + row - ROWS
            return flat[1][pl.ds(start, LOCAL, stride=FIELDS * HALO), :]
        return x_ref[pl.ds(field * ROWS + row, LOCAL, stride=FIELDS * ROWS), :]

    first, last = space == 0, space == SPACES - 1

    def outside(row):
        return first if row < 0 else last if row >= ROWS else None

    forecast = Forecast(load, outside)

    def block_copy(k):
        return pltpu.make_async_remote_copy(
            src_ref=sendbuf.at[k],
            dst_ref=values_ref.at[me],
            send_sem=a2a_send.at[k],
            recv_sem=a2a_recv.at[me],
            device_id=owner_id(k),
            device_id_type=MESH,
        )

    def emit(rows):
        for row in rows:
            for field in range(FIELDS):
                sendbuf[row, :, field * COLS : (field + 1) * COLS] = forecast.get(
                    field, STEPS, row
                )

    def start(k):
        @pl.when(k != me)
        def _():
            block_copy(k).start()

    inner = ROWS - 2 * HALO
    emit(range(HALO, ROWS - HALO))
    for d in range(inner):
        start(HALO + lax.rem(me + d, inner))
    up.wait()
    down.wait()
    emit(list(range(HALO)) + list(range(ROWS - HALO, ROWS)))
    for d in range(2 * HALO):
        start(lax.rem(ROWS - HALO + lax.rem(me + d, 2 * HALO), ROWS))
    values_ref[me] = sendbuf[me]
    for d in range(1, OWNERS):
        block_copy(lax.rem(me + d, OWNERS)).wait_send()
    for d in range(1, OWNERS):
        k = lax.rem(me + d, OWNERS)
        pltpu.make_async_remote_copy(
            src_ref=sendbuf.at[k],
            dst_ref=values_ref.at[k],
            send_sem=a2a_send.at[k],
            recv_sem=a2a_recv.at[k],
            device_id=owner_id(k),
            device_id_type=MESH,
        ).wait_recv()

    values = values_ref[...].reshape(ENSEMBLE, CELLS)
    mean = jnp.sum(values, axis=0, keepdims=True) * (1.0 / ENSEMBLE)
    scaled = (values - mean) * weight
    innovation = weight * (seen_value - mean)
    gram = dot_nt(scaled, scaled)
    pull = dot_nt(jnp.broadcast_to(innovation, (8, CELLS)), scaled)[0:1, :]
    left, right = gram[:, :COLS], gram[:, COLS:]
    mine[0] = left
    mine[1] = right
    mine[1, 0:1, :] = pull[:, :COLS]
    mine[1, 1:2, :] = pull[:, COLS:]

    def exchange(src, dst, sem_pair, slot_send, slot_recv, device):
        copy = pltpu.make_async_remote_copy(
            src_ref=src,
            dst_ref=dst,
            send_sem=sem_pair.at[0, slot_send],
            recv_sem=sem_pair.at[1, slot_recv],
            device_id=device,
            device_id_type=MESH,
        )
        copy.start()
        return copy

    partner = {"member": member + 1 - 2 * core}
    copy = exchange(mine.at[1 - core], corebuf, core_sem, 0, 0, partner)
    copy.wait()
    half = mine[core] + corebuf[...]
    x_to[...] = half.reshape(GROUPS, ENSEMBLE // GROUPS, COLS)

    copies = []
    for d in range(1, GROUPS):
        there = lax.rem(group + d, GROUPS)
        copies.append(
            exchange(x_to.at[there], x_from.at[d - 1], x_sem, d - 1, d - 1, {"group": there})
        )
    for copy in copies:
        copy.wait()
    quarter = x_to[group] + (x_from[0] + x_from[1] + x_from[2])
    y_to[...] = quarter.reshape(NY_CHIPS, 8, COLS)

    copies = []
    for d in range(1, NY_CHIPS):
        there = lax.rem(y + d, NY_CHIPS)
        copies.append(
            exchange(y_to.at[there], y_from.at[d - 1], y_sem, d - 1, d - 1, y_peers[d - 1])
        )
    for copy in copies:
        copy.wait()
    tile = y_to[y]
    for d in range(1, NY_CHIPS):
        tile = tile + y_from[d - 1]

    z_own[...] = tile
    z_from[z] = tile
    copies = []
    for d in range(1, NZ):
        copies.append(exchange(z_own, z_from.at[z], z_sem, d - 1, d - 1, z_peers[d - 1]))
    for copy in copies:
        copy.wait()
    total = z_from[0]
    for at in range(1, NZ):
        total = total + z_from[at]

    all_y[y] = total
    copies = []
    for d in range(1, NY_CHIPS):
        copies.append(
            exchange(all_y.at[y], all_y.at[y], gy_sem, d - 1, d - 1, y_peers[d - 1])
        )
    for copy in copies:
        copy.wait()

    x_slice = all_y[...].reshape(ENSEMBLE // GROUPS, COLS)
    all_x[group] = x_slice
    copies = []
    for d in range(1, GROUPS):
        there = lax.rem(group + d, GROUPS)
        copies.append(
            exchange(all_x.at[group], all_x.at[group], gx_sem, d - 1, d - 1, {"group": there})
        )
    for copy in copies:
        copy.wait()

    gram_ref[core] = all_x[...].reshape(ENSEMBLE, COLS)
    copy = exchange(gram_ref.at[core], gram_ref.at[core], gc_sem, 0, 0, partner)
    copy.wait()


STEPS = 2


def gather(state, obs, index):
    vmem = pl.BlockSpec(memory_space=pltpu.VMEM)
    dma = pltpu.SemaphoreType.DMA
    quarter = ENSEMBLE // GROUPS
    return pl.pallas_call(
        gather_kernel,
        out_shape=(
            jax.ShapeDtypeStruct((OWNERS, LOCAL, CELLS), F32),
            jax.ShapeDtypeStruct((2, ENSEMBLE, COLS), F32),
        ),
        in_specs=[vmem, pl.BlockSpec(memory_space=pl.ANY), vmem, vmem],
        out_specs=(vmem, vmem),
        scratch_shapes=[
            pltpu.VMEM((2, LOCAL * FIELDS, HALO, COLS), F32),
            pltpu.VMEM((OWNERS, LOCAL, CELLS), F32),
            pltpu.VMEM((2, ENSEMBLE, COLS), F32),
            pltpu.VMEM((ENSEMBLE, COLS), F32),
            pltpu.VMEM((GROUPS - 1, quarter, COLS), F32),
            pltpu.VMEM((GROUPS, quarter, COLS), F32),
            pltpu.VMEM((NY_CHIPS - 1, 8, COLS), F32),
            pltpu.VMEM((NY_CHIPS, 8, COLS), F32),
            pltpu.VMEM((NZ, 8, COLS), F32),
            pltpu.VMEM((8, COLS), F32),
            pltpu.VMEM((NY_CHIPS, 8, COLS), F32),
            pltpu.VMEM((GROUPS, quarter, COLS), F32),
            dma((2,)),
            dma((2,)),
            dma((OWNERS,)),
            dma((OWNERS,)),
            dma((2, 1)),
            dma((2, GROUPS - 1)),
            dma((2, NY_CHIPS - 1)),
            dma((2, NZ - 1)),
            dma((2, NY_CHIPS - 1)),
            dma((2, GROUPS - 1)),
            dma((2, 1)),
        ],
        compiler_params=pltpu.CompilerParams(collective_id=0, has_side_effects=True),
        name="gather_and_gram",
    )(
        state.reshape(LOCAL * FIELDS * ROWS, COLS),
        state.reshape(LOCAL * FIELDS, ROWS // HALO, HALO, COLS),
        obs,
        index,
    )


def return_kernel(values_ref, transform_ref, out_ref, sendbuf, arrived, send_sem, recv_sem):
    group, member, _ = place()
    me = group * MEMBERS + member
    barrier = pltpu.get_barrier_semaphore()
    for d in range(1, OWNERS):
        pl.semaphore_signal(
            barrier, inc=1, device_id=owner_id(lax.rem(me + d, OWNERS)), device_id_type=MESH
        )
    values = values_ref[...].reshape(ENSEMBLE, CELLS)
    mean = jnp.sum(values, axis=0, keepdims=True) * (1.0 / ENSEMBLE)
    updated = dot_nn(transform_ref[...], values - mean) + mean
    sendbuf[...] = updated.reshape(OWNERS, LOCAL, CELLS)
    pl.semaphore_wait(barrier, OWNERS - 1)

    def copy(k, slot):
        return pltpu.make_async_remote_copy(
            src_ref=sendbuf.at[k],
            dst_ref=arrived.at[slot],
            send_sem=send_sem.at[k],
            recv_sem=recv_sem.at[slot],
            device_id=owner_id(k),
            device_id_type=MESH,
        )

    for d in range(1, OWNERS):
        copy(lax.rem(me + d, OWNERS), me).start()
    arrived[me] = sendbuf[me]
    for d in range(1, OWNERS):
        copy(lax.rem(me + d, OWNERS), me).wait_send()
    for d in range(1, OWNERS):
        k = lax.rem(me + d, OWNERS)
        copy(k, k).wait_recv()
    for row in range(ROWS):
        for field in range(FIELDS):
            out_ref[pl.ds(field * ROWS + row, LOCAL, stride=FIELDS * ROWS), :] = arrived[
                row, :, field * COLS : (field + 1) * COLS
            ]


def give_back(values, transform):
    vmem = pl.BlockSpec(memory_space=pltpu.VMEM)
    dma = pltpu.SemaphoreType.DMA
    out = pl.pallas_call(
        return_kernel,
        out_shape=jax.ShapeDtypeStruct((LOCAL * FIELDS * ROWS, COLS), F32),
        in_specs=[vmem, vmem],
        out_specs=vmem,
        scratch_shapes=[
            pltpu.VMEM((OWNERS, LOCAL, CELLS), F32),
            pltpu.VMEM((OWNERS, LOCAL, CELLS), F32),
            dma((OWNERS,)),
            dma((OWNERS,)),
        ],
        compiler_params=pltpu.CompilerParams(collective_id=1, has_side_effects=True),
        name="update_and_return",
    )(values, transform)
    return out.reshape(LOCAL, FIELDS, ROWS, COLS)


def make_transform(both):
    pull = jnp.concatenate([both[1, 0], both[1, 1]])
    corner = jnp.zeros((COLS, COLS), F32)
    upper = jnp.concatenate([both[0, :COLS], corner], axis=1)
    lower = jnp.concatenate([both[0, COLS:], both[1, COLS:]], axis=1)
    gram = jnp.concatenate([upper, lower], axis=0)
    identity = jnp.eye(ENSEMBLE, dtype=F32)
    factor = lax.linalg.cholesky(identity + gram, symmetrize_input=False)
    inverse = jax.scipy.linalg.solve_triangular(factor, identity, lower=True)
    inner = jnp.dot(inverse, pull, precision=HIGHEST)
    weights_mean = jnp.dot(inverse.T, inner, precision=HIGHEST)
    return inverse + weights_mean[None, :]


def on_device(height_velocity_tensor, obs_values, obs_precision, obs_index):
    obs = jnp.concatenate([obs_values, obs_precision, jnp.zeros((6, OBS), F32)], axis=0)
    values, both = gather(height_velocity_tensor, obs, obs_index)
    return give_back(values, make_transform(both))


def solution(mesh):
    return jax.shard_map(
        on_device,
        mesh=mesh,
        in_specs=(
            P(("group", "member"), None, "space", None),
            P(("group", "member", "space"), None),
            P(("group", "member", "space"), None),
            P(("group", "member", "space"), None),
        ),
        out_specs=P(("group", "member"), None, "space", None),
        check_vma=False,
    )
```

```python
import math

import jax
import jax.numpy as jnp
from jax import lax
from jax.experimental import pallas as pl
from jax.experimental.pallas import tpu as pltpu
from jax.sharding import PartitionSpec as P

GRAV = 0.4
DEPTH = 0.4
GROUPS, MEMBERS, SPACES = 4, 8, 24
NZ, NY_CHIPS = 12, 8
OWNERS = GROUPS * MEMBERS
ROWS = 32
LOCAL = 8
ENSEMBLE = OWNERS * LOCAL
FIELDS = 3
COLS = 128
CELLS = FIELDS * COLS
OBS = 192
HALO = 4
BLOCK, SUB = 64, 8
MESH = pl.DeviceIdType.MESH
F32 = jnp.float32
HIGHEST = lax.Precision.HIGHEST
SCALE = 1.0 / math.sqrt(ENSEMBLE - 1)


def dot_nt(a, b):
    return lax.dot_general(
        a, b, (((1,), (1,)), ((), ())), precision=HIGHEST, preferred_element_type=F32
    )


def dot_nn(a, b):
    return lax.dot_general(
        a, b, (((1,), (0,)), ((), ())), precision=HIGHEST, preferred_element_type=F32
    )


def place():
    group = lax.axis_index("group")
    member = lax.axis_index("member")
    space = lax.axis_index("space")
    return group, member, space


def owner_id(k):
    return {"group": k // MEMBERS, "member": lax.rem(k, MEMBERS)}


def z_id(z, core, y):
    return {"member": z // 3 * 2 + core, "space": lax.rem(z, 3) * NY_CHIPS + y}


def across_y(field):
    return pltpu.roll(field, COLS - 1, 1) - pltpu.roll(field, 1, 1)


class Forecast:
    def __init__(self, load, outside):
        self.load = load
        self.outside = outside
        self.known = {}

    def masked(self, row, value):
        flag = self.outside(row)
        return value if flag is None else jnp.where(flag, 0.0, value)

    def get(self, field, step, row):
        key = (field, step, row)
        if key not in self.known:
            self.known[key] = self.compute(field, step, row)
        return self.known[key]

    def compute(self, field, step, row):
        if step == 0:
            return self.masked(row, self.load(field, row))
        if field == 1:
            ahead, behind = self.get(0, step - 1, row + 1), self.get(0, step - 1, row - 1)
            return self.masked(row, self.get(1, step - 1, row) - GRAV * (ahead - behind))
        if field == 2:
            return self.get(2, step - 1, row) - GRAV * across_y(self.get(0, step - 1, row))
        ahead, behind = self.get(1, step, row + 1), self.get(1, step, row - 1)
        change = ahead - behind + across_y(self.get(2, step, row))
        return self.masked(row, self.get(0, step - 1, row) - DEPTH * change)


def gather_kernel(
    x_ref,
    x_halo_ref,
    obs_ref,
    index_ref,
    values_ref,
    gram_ref,
    halo,
    sendbuf,
    mine,
    corebuf,
    x_from,
    x_to,
    y_from,
    y_to,
    z_from,
    z_own,
    all_y,
    all_x,
    halo_send,
    halo_recv,
    a2a_send,
    a2a_recv,
    core_sem,
    x_sem,
    y_sem,
    z_sem,
    gy_sem,
    gx_sem,
    gc_sem,
):
    group, member, space = place()
    core = lax.rem(member, 2)
    z = member // 2 * 3 + space // NY_CHIPS
    y = lax.rem(space, NY_CHIPS)
    me = group * MEMBERS + member

    barrier = pltpu.get_barrier_semaphore()
    above, below = lax.rem(space + SPACES - 1, SPACES), lax.rem(space + 1, SPACES)
    peers = [{"space": above}, {"space": below}]
    peers += [owner_id(lax.rem(me + d, OWNERS)) for d in range(1, OWNERS)]
    y_peers = [
        {"space": space - y + lax.rem(y + d, NY_CHIPS)} for d in range(1, NY_CHIPS)
    ]
    z_peers = [z_id(lax.rem(z + d, NZ), core, y) for d in range(1, NZ)]
    peers += y_peers + z_peers
    for peer in peers:
        pl.semaphore_signal(barrier, inc=1, device_id=peer, device_id_type=MESH)

    cells = lax.broadcasted_iota(jnp.int32, (CELLS, OBS), 0)
    picked = jnp.where(cells == index_ref[0:1, :], 1.0, 0.0)
    spread = dot_nt(obs_ref[...], picked)
    weight = spread[1:2, :] * SCALE
    seen_value = spread[0:1, :]

    pl.semaphore_wait(barrier, len(peers))

    up = pltpu.make_async_remote_copy(
        src_ref=x_halo_ref.at[:, 0],
        dst_ref=halo.at[1],
        send_sem=halo_send.at[0],
        recv_sem=halo_recv.at[1],
        device_id={"space": above},
        device_id_type=MESH,
    )
    down = pltpu.make_async_remote_copy(
        src_ref=x_halo_ref.at[:, ROWS // HALO - 1],
        dst_ref=halo.at[0],
        send_sem=halo_send.at[1],
        recv_sem=halo_recv.at[0],
        device_id={"space": below},
        device_id_type=MESH,
    )
    up.start()
    down.start()

    flat = [halo.at[i].reshape(LOCAL * FIELDS * HALO, COLS) for i in range(2)]

    def load(field, row):
        if row < 0:
            start = field * HALO + row + HALO
            return flat[0][pl.ds(start, LOCAL, stride=FIELDS * HALO), :]
        if row >= ROWS:
            start = field * HALO + row - ROWS
            return flat[1][pl.ds(start, LOCAL, stride=FIELDS * HALO), :]
        return x_ref[pl.ds(field * ROWS + row, LOCAL, stride=FIELDS * ROWS), :]

    first, last = space == 0, space == SPACES - 1

    def outside(row):
        return first if row < 0 else last if row >= ROWS else None

    forecast = Forecast(load, outside)

    def block_copy(k):
        return pltpu.make_async_remote_copy(
            src_ref=sendbuf.at[k],
            dst_ref=values_ref.at[me],
            send_sem=a2a_send.at[k],
            recv_sem=a2a_recv.at[me],
            device_id=owner_id(k),
            device_id_type=MESH,
        )

    def emit(rows):
        for row in rows:
            for field in range(FIELDS):
                sendbuf[row, :, field * COLS : (field + 1) * COLS] = forecast.get(
                    field, STEPS, row
                )

    def start(k):
        @pl.when(k != me)
        def _():
            block_copy(k).start()

    inner = ROWS - 2 * HALO
    emit(range(HALO, ROWS - HALO))
    for d in range(inner):
        start(HALO + lax.rem(me + d, inner))
    up.wait()
    down.wait()
    emit(list(range(HALO)) + list(range(ROWS - HALO, ROWS)))
    for d in range(2 * HALO):
        start(lax.rem(ROWS - HALO + lax.rem(me + d, 2 * HALO), ROWS))
    values_ref[me] = sendbuf[me]
    for d in range(1, OWNERS):
        block_copy(lax.rem(me + d, OWNERS)).wait_send()
    for d in range(1, OWNERS):
        k = lax.rem(me + d, OWNERS)
        pltpu.make_async_remote_copy(
            src_ref=sendbuf.at[k],
            dst_ref=values_ref.at[k],
            send_sem=a2a_send.at[k],
            recv_sem=a2a_recv.at[k],
            device_id=owner_id(k),
            device_id_type=MESH,
        ).wait_recv()

    values = values_ref[...].reshape(ENSEMBLE, CELLS)
    mean = jnp.sum(values, axis=0, keepdims=True) * (1.0 / ENSEMBLE)
    scaled = (values - mean) * weight
    innovation = weight * (seen_value - mean)
    gram = dot_nt(scaled, scaled)
    pull = dot_nt(jnp.broadcast_to(innovation, (8, CELLS)), scaled)[0:1, :]
    left, right = gram[:, :COLS], gram[:, COLS:]
    mine[0] = left
    mine[1] = right
    mine[1, 0:1, :] = pull[:, :COLS]
    mine[1, 1:2, :] = pull[:, COLS:]

    def exchange(src, dst, sem_pair, slot_send, slot_recv, device):
        copy = pltpu.make_async_remote_copy(
            src_ref=src,
            dst_ref=dst,
            send_sem=sem_pair.at[0, slot_send],
            recv_sem=sem_pair.at[1, slot_recv],
            device_id=device,
            device_id_type=MESH,
        )
        copy.start()
        return copy

    partner = {"member": member + 1 - 2 * core}
    copy = exchange(mine.at[1 - core], corebuf, core_sem, 0, 0, partner)
    copy.wait()
    half = mine[core] + corebuf[...]
    x_to[...] = half.reshape(GROUPS, ENSEMBLE // GROUPS, COLS)

    copies = []
    for d in range(1, GROUPS):
        there = lax.rem(group + d, GROUPS)
        copies.append(
            exchange(x_to.at[there], x_from.at[d - 1], x_sem, d - 1, d - 1, {"group": there})
        )
    for copy in copies:
        copy.wait()
    quarter = x_to[group] + (x_from[0] + x_from[1] + x_from[2])
    y_to[...] = quarter.reshape(NY_CHIPS, 8, COLS)

    copies = []
    for d in range(1, NY_CHIPS):
        there = lax.rem(y + d, NY_CHIPS)
        copies.append(
            exchange(y_to.at[there], y_from.at[d - 1], y_sem, d - 1, d - 1, y_peers[d - 1])
        )
    for copy in copies:
        copy.wait()
    tile = y_to[y]
    for d in range(1, NY_CHIPS):
        tile = tile + y_from[d - 1]

    z_own[...] = tile
    z_from[z] = tile
    copies = []
    for d in range(1, NZ):
        copies.append(exchange(z_own, z_from.at[z], z_sem, d - 1, d - 1, z_peers[d - 1]))
    for copy in copies:
        copy.wait()
    total = z_from[0]
    for at in range(1, NZ):
        total = total + z_from[at]

    all_y[y] = total
    copies = []
    for d in range(1, NY_CHIPS):
        copies.append(
            exchange(all_y.at[y], all_y.at[y], gy_sem, d - 1, d - 1, y_peers[d - 1])
        )
    for copy in copies:
        copy.wait()

    x_slice = all_y[...].reshape(ENSEMBLE // GROUPS, COLS)
    all_x[group] = x_slice
    copies = []
    for d in range(1, GROUPS):
        there = lax.rem(group + d, GROUPS)
        copies.append(
            exchange(all_x.at[group], all_x.at[group], gx_sem, d - 1, d - 1, {"group": there})
        )
    for copy in copies:
        copy.wait()

    gram_ref[core] = all_x[...].reshape(ENSEMBLE, COLS)
    copy = exchange(gram_ref.at[core], gram_ref.at[core], gc_sem, 0, 0, partner)
    copy.wait()


STEPS = 2


def gather(state, obs, index):
    vmem = pl.BlockSpec(memory_space=pltpu.VMEM)
    dma = pltpu.SemaphoreType.DMA
    quarter = ENSEMBLE // GROUPS
    return pl.pallas_call(
        gather_kernel,
        out_shape=(
            jax.ShapeDtypeStruct((OWNERS, LOCAL, CELLS), F32),
            jax.ShapeDtypeStruct((2, ENSEMBLE, COLS), F32),
        ),
        in_specs=[vmem, pl.BlockSpec(memory_space=pl.ANY), vmem, vmem],
        out_specs=(vmem, vmem),
        scratch_shapes=[
            pltpu.VMEM((2, LOCAL * FIELDS, HALO, COLS), F32),
            pltpu.VMEM((OWNERS, LOCAL, CELLS), F32),
            pltpu.VMEM((2, ENSEMBLE, COLS), F32),
            pltpu.VMEM((ENSEMBLE, COLS), F32),
            pltpu.VMEM((GROUPS - 1, quarter, COLS), F32),
            pltpu.VMEM((GROUPS, quarter, COLS), F32),
            pltpu.VMEM((NY_CHIPS - 1, 8, COLS), F32),
            pltpu.VMEM((NY_CHIPS, 8, COLS), F32),
            pltpu.VMEM((NZ, 8, COLS), F32),
            pltpu.VMEM((8, COLS), F32),
            pltpu.VMEM((NY_CHIPS, 8, COLS), F32),
            pltpu.VMEM((GROUPS, quarter, COLS), F32),
            dma((2,)),
            dma((2,)),
            dma((OWNERS,)),
            dma((OWNERS,)),
            dma((2, 1)),
            dma((2, GROUPS - 1)),
            dma((2, NY_CHIPS - 1)),
            dma((2, NZ - 1)),
            dma((2, NY_CHIPS - 1)),
            dma((2, GROUPS - 1)),
            dma((2, 1)),
        ],
        compiler_params=pltpu.CompilerParams(collective_id=0, has_side_effects=True),
        name="gather_and_gram",
    )(
        state.reshape(LOCAL * FIELDS * ROWS, COLS),
        state.reshape(LOCAL * FIELDS, ROWS // HALO, HALO, COLS),
        obs,
        index,
    )


def return_kernel(values_ref, transform_ref, out_ref, sendbuf, arrived, send_sem, recv_sem):
    group, member, _ = place()
    me = group * MEMBERS + member
    barrier = pltpu.get_barrier_semaphore()
    for d in range(1, OWNERS):
        pl.semaphore_signal(
            barrier, inc=1, device_id=owner_id(lax.rem(me + d, OWNERS)), device_id_type=MESH
        )
    values = values_ref[...].reshape(ENSEMBLE, CELLS)
    mean = jnp.sum(values, axis=0, keepdims=True) * (1.0 / ENSEMBLE)
    updated = dot_nn(transform_ref[...], values - mean) + mean
    sendbuf[...] = updated.reshape(OWNERS, LOCAL, CELLS)
    pl.semaphore_wait(barrier, OWNERS - 1)

    def copy(k, slot):
        return pltpu.make_async_remote_copy(
            src_ref=sendbuf.at[k],
            dst_ref=arrived.at[slot],
            send_sem=send_sem.at[k],
            recv_sem=recv_sem.at[slot],
            device_id=owner_id(k),
            device_id_type=MESH,
        )

    for d in range(1, OWNERS):
        copy(lax.rem(me + d, OWNERS), me).start()
    arrived[me] = sendbuf[me]
    for d in range(1, OWNERS):
        copy(lax.rem(me + d, OWNERS), me).wait_send()
    for d in range(1, OWNERS):
        k = lax.rem(me + d, OWNERS)
        copy(k, k).wait_recv()
    for row in range(ROWS):
        for field in range(FIELDS):
            out_ref[pl.ds(field * ROWS + row, LOCAL, stride=FIELDS * ROWS), :] = arrived[
                row, :, field * COLS : (field + 1) * COLS
            ]


def give_back(values, transform):
    vmem = pl.BlockSpec(memory_space=pltpu.VMEM)
    dma = pltpu.SemaphoreType.DMA
    out = pl.pallas_call(
        return_kernel,
        out_shape=jax.ShapeDtypeStruct((LOCAL * FIELDS * ROWS, COLS), F32),
        in_specs=[vmem, vmem],
        out_specs=vmem,
        scratch_shapes=[
            pltpu.VMEM((OWNERS, LOCAL, CELLS), F32),
            pltpu.VMEM((OWNERS, LOCAL, CELLS), F32),
            dma((OWNERS,)),
            dma((OWNERS,)),
        ],
        compiler_params=pltpu.CompilerParams(collective_id=1, has_side_effects=True),
        name="update_and_return",
    )(values, transform)
    return out.reshape(LOCAL, FIELDS, ROWS, COLS)


def lane(tile, at):
    return jnp.broadcast_to(tile[:, at : at + 1], (SUB, COLS))

def sublane(tile, at):
    return jnp.broadcast_to(tile[at : at + 1, :], (SUB, COLS))

def total(terms):
    while len(terms) > 1:
        terms = [a + b for a, b in zip(terms[::2], terms[1::2])] + (
            [terms[-1]] if len(terms) % 2 else []
        )
    return terms[0]

def small_factor(tile, at):
    columns = [lane(tile, at + j) for j in range(SUB)]
    left = {(i, j): sublane(columns[j], i) for j in range(SUB) for i in range(j, SUB)}
    low, inv = {}, {}
    for j in range(SUB):
        root = lax.rsqrt(left[j, j])
        inv[j, j] = root
        for i in range(j + 1, SUB):
            low[i, j] = left[i, j] * root
        for k in range(j + 1, SUB):
            for i in range(k, SUB):
                left[i, k] = left[i, k] - low[i, j] * low[k, j]
    for j in range(SUB):
        for i in range(j + 1, SUB):
            terms = [low[i, k] * inv[k, j] for k in range(j, i)]
            inv[i, j] = -(total(terms) * inv[i, i])
    return inv

def invert_block(block, identity):
    wide = jnp.concatenate([block, identity], axis=1)
    tiles = [wide[SUB * q : SUB * (q + 1)] for q in range(BLOCK // SUB)]
    rows = lax.broadcasted_iota(jnp.int32, (SUB, COLS), 0)
    count = len(tiles)
    for p in range(count):
        inv = small_factor(tiles[p], SUB * p)
        terms = []
        for j in range(SUB):
            column = inv[SUB - 1, j]
            for i in range(SUB - 2, j - 1, -1):
                column = jnp.where(rows <= i, inv[i, j], column)
            if j > 0:
                column = jnp.where(rows < j, 0.0, column)
            terms.append(column * sublane(tiles[p], j))
        done = total(terms)
        spread = [sublane(done, k) for k in range(SUB)]
        for q in range(p + 1, count):
            source = [lane(tiles[q], SUB * p + j) for j in range(SUB)]
            terms = [
                total([inv[k, j] * source[j] for j in range(k + 1)]) * spread[k]
                for k in range(SUB)
            ]
            tiles[q] = tiles[q] - total(terms)
        tiles[p] = done
    return jnp.concatenate(tiles, axis=0)[:, BLOCK:]

def invert(work):
    n = ENSEMBLE // BLOCK
    r = lax.broadcasted_iota(jnp.int32, (BLOCK, BLOCK), 0)
    c = lax.broadcasted_iota(jnp.int32, (BLOCK, BLOCK), 1)
    identity = jnp.where(r == c, 1.0, 0.0)
    zero = jnp.zeros((BLOCK, BLOCK), F32)
    for k in range(n):
        at = k * BLOCK
        own = slice(at, at + BLOCK)
        rest = slice(at + BLOCK, ENSEMBLE)
        inverse = invert_block(work[own, own], identity)
        if k < n - 1:
            factor = dot_nt(work[rest, own], inverse)
        work[own, own] = identity
        solved = dot_nn(inverse, work[own, :])
        work[own, :] = solved
        if k < n - 1:
            work[rest, own] = jnp.zeros((ENSEMBLE - at - BLOCK, BLOCK), F32)
            work[rest, :] = work[rest, :] - dot_nn(factor, solved)

def transform_kernel(both_ref, transform_ref, work):
    r = lax.broadcasted_iota(jnp.int32, (COLS, COLS), 0)
    c = lax.broadcasted_iota(jnp.int32, (COLS, COLS), 1)
    eye = jnp.where(r == c, 1.0, 0.0)
    below = both_ref[0, COLS:, :]
    work[:COLS, :COLS] = both_ref[0, :COLS, :] + eye
    work[COLS:, :COLS] = below
    work[:COLS, COLS:] = below.T
    work[COLS:, COLS:] = both_ref[1, COLS:, :] + eye
    pull = jnp.concatenate([both_ref[1, 0:1, :], both_ref[1, 1:2, :]], axis=1)
    invert(work)
    r = lax.broadcasted_iota(jnp.int32, (ENSEMBLE, ENSEMBLE), 0)
    c = lax.broadcasted_iota(jnp.int32, (ENSEMBLE, ENSEMBLE), 1)
    inverse = jnp.where(r >= c, work[...], 0.0)
    inner = dot_nt(jnp.broadcast_to(pull, (SUB, ENSEMBLE)), inverse)
    weights = dot_nn(inner, inverse)
    transform_ref[...] = inverse + weights[0:1, :]


def make_transform(both):
    vmem = pl.BlockSpec(memory_space=pltpu.VMEM)
    return pl.pallas_call(
        transform_kernel,
        out_shape=jax.ShapeDtypeStruct((ENSEMBLE, ENSEMBLE), F32),
        in_specs=[vmem],
        out_specs=vmem,
        scratch_shapes=[pltpu.VMEM((ENSEMBLE, ENSEMBLE), F32)],
        name="factor_and_invert",
    )(both)


def on_device(height_velocity_tensor, obs_values, obs_precision, obs_index):
    obs = jnp.concatenate([obs_values, obs_precision, jnp.zeros((6, OBS), F32)], axis=0)
    values, both = gather(height_velocity_tensor, obs, obs_index)
    return give_back(values, make_transform(both))


def solution(mesh):
    return jax.shard_map(
        on_device,
        mesh=mesh,
        in_specs=(
            P(("group", "member"), None, "space", None),
            P(("group", "member", "space"), None),
            P(("group", "member", "space"), None),
            P(("group", "member", "space"), None),
        ),
        out_specs=P(("group", "member"), None, "space", None),
        check_vma=False,
    )
```

```python
import math

import jax
import jax.numpy as jnp
from jax import lax
from jax.experimental import pallas as pl
from jax.experimental.pallas import tpu as pltpu
from jax.sharding import PartitionSpec as P

GRAV = 0.4
DEPTH = 0.4
GROUPS, MEMBERS, SPACES = 4, 8, 24
NZ, NY_CHIPS = 12, 8
OWNERS = GROUPS * MEMBERS
ROWS = 32
LOCAL = 8
ENSEMBLE = OWNERS * LOCAL
FIELDS = 3
COLS = 128
CELLS = FIELDS * COLS
OBS = 192
HALO = 4
BLOCK, SUB = 64, 8
MESH = pl.DeviceIdType.MESH
F32 = jnp.float32
HIGHEST = lax.Precision.HIGHEST
SCALE = 1.0 / math.sqrt(ENSEMBLE - 1)


def dot_nt(a, b):
    return lax.dot_general(
        a, b, (((1,), (1,)), ((), ())), precision=HIGHEST, preferred_element_type=F32
    )


def dot_nn(a, b):
    return lax.dot_general(
        a, b, (((1,), (0,)), ((), ())), precision=HIGHEST, preferred_element_type=F32
    )


def place():
    group = lax.axis_index("group")
    member = lax.axis_index("member")
    space = lax.axis_index("space")
    return group, member, space


def owner_id(k):
    return {"group": k // MEMBERS, "member": lax.rem(k, MEMBERS)}


def hops(offset):
    return min(offset[0], GROUPS - offset[0]) + 3 * min(offset[1], 4 - offset[1])


OFFSETS = sorted(
    [(a, b, c) for a in range(GROUPS) for b in range(4) for c in range(2) if a + b + c],
    key=hops,
    reverse=True,
)


def other_owners(group, member):
    z_part, core = member // 2, lax.rem(member, 2)
    for a, b, c in OFFSETS:
        there = lax.rem(group + a, GROUPS) * MEMBERS
        yield there + lax.rem(z_part + b, 4) * 2 + lax.rem(core + c, 2)


def z_id(z, core, y):
    return {"member": z // 3 * 2 + core, "space": lax.rem(z, 3) * NY_CHIPS + y}


def across_y(field):
    return pltpu.roll(field, COLS - 1, 1) - pltpu.roll(field, 1, 1)


class Forecast:
    def __init__(self, load, outside):
        self.load = load
        self.outside = outside
        self.known = {}

    def masked(self, row, value):
        flag = self.outside(row)
        return value if flag is None else jnp.where(flag, 0.0, value)

    def get(self, field, step, row):
        key = (field, step, row)
        if key not in self.known:
            self.known[key] = self.compute(field, step, row)
        return self.known[key]

    def compute(self, field, step, row):
        if step == 0:
            return self.masked(row, self.load(field, row))
        if field == 1:
            ahead, behind = self.get(0, step - 1, row + 1), self.get(0, step - 1, row - 1)
            return self.masked(row, self.get(1, step - 1, row) - GRAV * (ahead - behind))
        if field == 2:
            return self.get(2, step - 1, row) - GRAV * across_y(self.get(0, step - 1, row))
        ahead, behind = self.get(1, step, row + 1), self.get(1, step, row - 1)
        change = ahead - behind + across_y(self.get(2, step, row))
        return self.masked(row, self.get(0, step - 1, row) - DEPTH * change)


def gather_kernel(
    x_hbm_ref,
    x_halo_ref,
    value_ref,
    precision_ref,
    index_ref,
    values_ref,
    gram_ref,
    x_ref,
    halo,
    sendbuf,
    mine,
    corebuf,
    x_from,
    x_to,
    y_from,
    y_to,
    z_from,
    z_own,
    all_y,
    all_x,
    x_in_sem,
    halo_send,
    halo_recv,
    a2a_send,
    a2a_recv,
    core_sem,
    x_sem,
    y_sem,
    z_sem,
    gy_sem,
    gx_sem,
    gc_sem,
):
    group, member, space = place()
    core = lax.rem(member, 2)
    z = member // 2 * 3 + space // NY_CHIPS
    y = lax.rem(space, NY_CHIPS)
    me = group * MEMBERS + member

    x_in = pltpu.make_async_copy(x_hbm_ref, x_ref, x_in_sem)
    x_in.start()

    barrier = pltpu.get_barrier_semaphore()
    above, below = lax.rem(space + SPACES - 1, SPACES), lax.rem(space + 1, SPACES)
    peers = [{"space": above}, {"space": below}]
    owners = list(other_owners(group, member))
    peers += [owner_id(k) for k in owners]
    y_peers = [
        {"space": space - y + lax.rem(y + d, NY_CHIPS)} for d in range(1, NY_CHIPS)
    ]
    z_peers = [z_id(lax.rem(z + d, NZ), core, y) for d in range(1, NZ)]
    peers += y_peers + z_peers
    for peer in peers:
        pl.semaphore_signal(barrier, inc=1, device_id=peer, device_id_type=MESH)

    cells = lax.broadcasted_iota(jnp.int32, (CELLS, OBS), 0)
    picked = jnp.where(cells == index_ref[0:1, :], 1.0, 0.0)
    spread = dot_nt(jnp.broadcast_to(precision_ref[...], (SUB, OBS)), picked)
    weight = spread[0:1, :] * SCALE
    spread = dot_nt(jnp.broadcast_to(value_ref[...], (SUB, OBS)), picked)
    seen_value = spread[0:1, :]

    flat = [halo.at[i].reshape(LOCAL * FIELDS * HALO, COLS) for i in range(2)]

    def load(field, row):
        if row < 0:
            start = field * HALO + row + HALO
            return flat[0][pl.ds(start, LOCAL, stride=FIELDS * HALO), :]
        if row >= ROWS:
            start = field * HALO + row - ROWS
            return flat[1][pl.ds(start, LOCAL, stride=FIELDS * HALO), :]
        return x_ref[pl.ds(field * ROWS + row, LOCAL, stride=FIELDS * ROWS), :]

    first, last = space == 0, space == SPACES - 1

    def outside(row):
        return first if row < 0 else last if row >= ROWS else None

    forecast = Forecast(load, outside)

    def block_copy(k):
        return pltpu.make_async_remote_copy(
            src_ref=sendbuf.at[k],
            dst_ref=values_ref.at[me],
            send_sem=a2a_send.at[k],
            recv_sem=a2a_recv.at[me],
            device_id=owner_id(k),
            device_id_type=MESH,
        )

    def emit(rows):
        for row in rows:
            for field in range(FIELDS):
                sendbuf[row, :, field * COLS : (field + 1) * COLS] = forecast.get(
                    field, STEPS, row
                )

    x_in.wait()
    emit(range(HALO, ROWS - HALO))
    pl.semaphore_wait(barrier, len(peers))

    up = pltpu.make_async_remote_copy(
        src_ref=x_halo_ref.at[:, 0],
        dst_ref=halo.at[1],
        send_sem=halo_send.at[0],
        recv_sem=halo_recv.at[1],
        device_id={"space": above},
        device_id_type=MESH,
    )
    down = pltpu.make_async_remote_copy(
        src_ref=x_halo_ref.at[:, ROWS // HALO - 1],
        dst_ref=halo.at[0],
        send_sem=halo_send.at[1],
        recv_sem=halo_recv.at[0],
        device_id={"space": below},
        device_id_type=MESH,
    )
    up.start()
    down.start()

    def is_inner(k):
        return jnp.logical_and(k >= HALO, k < ROWS - HALO)

    for k in owners:

        @pl.when(is_inner(k))
        def _():
            block_copy(k).start()

    up.wait()
    down.wait()
    emit(list(range(HALO)) + list(range(ROWS - HALO, ROWS)))
    for k in owners:

        @pl.when(jnp.logical_not(is_inner(k)))
        def _():
            block_copy(k).start()

    values_ref[me] = sendbuf[me]
    for k in owners:
        block_copy(k).wait_send()
    for k in owners:
        pltpu.make_async_remote_copy(
            src_ref=sendbuf.at[k],
            dst_ref=values_ref.at[k],
            send_sem=a2a_send.at[k],
            recv_sem=a2a_recv.at[k],
            device_id=owner_id(k),
            device_id_type=MESH,
        ).wait_recv()

    values = values_ref[...].reshape(ENSEMBLE, CELLS)
    mean = jnp.sum(values, axis=0, keepdims=True) * (1.0 / ENSEMBLE)
    scaled = (values - mean) * weight
    innovation = weight * (seen_value - mean)
    gram = dot_nt(scaled, scaled)
    pull = dot_nt(jnp.broadcast_to(innovation, (8, CELLS)), scaled)[0:1, :]
    left, right = gram[:, :COLS], gram[:, COLS:]
    mine[0] = left
    mine[1] = right
    mine[1, 0:1, :] = pull[:, :COLS]
    mine[1, 1:2, :] = pull[:, COLS:]

    def exchange(src, dst, sem_pair, slot_send, slot_recv, device):
        copy = pltpu.make_async_remote_copy(
            src_ref=src,
            dst_ref=dst,
            send_sem=sem_pair.at[0, slot_send],
            recv_sem=sem_pair.at[1, slot_recv],
            device_id=device,
            device_id_type=MESH,
        )
        copy.start()
        return copy

    partner = {"member": member + 1 - 2 * core}
    copy = exchange(mine.at[1 - core], corebuf, core_sem, 0, 0, partner)
    copy.wait()
    half = mine[core] + corebuf[...]
    x_to[...] = half.reshape(GROUPS, ENSEMBLE // GROUPS, COLS)

    copies = []
    for d in range(1, GROUPS):
        there = lax.rem(group + d, GROUPS)
        copies.append(
            exchange(x_to.at[there], x_from.at[d - 1], x_sem, d - 1, d - 1, {"group": there})
        )
    for copy in copies:
        copy.wait()
    quarter = x_to[group] + (x_from[0] + x_from[1] + x_from[2])
    y_to[...] = quarter.reshape(NY_CHIPS, 8, COLS)

    copies = []
    for d in range(1, NY_CHIPS):
        there = lax.rem(y + d, NY_CHIPS)
        copies.append(
            exchange(y_to.at[there], y_from.at[d - 1], y_sem, d - 1, d - 1, y_peers[d - 1])
        )
    for copy in copies:
        copy.wait()
    tile = y_to[y]
    for d in range(1, NY_CHIPS):
        tile = tile + y_from[d - 1]

    z_own[...] = tile
    z_from[z] = tile
    copies = []
    for d in range(1, NZ):
        copies.append(exchange(z_own, z_from.at[z], z_sem, d - 1, d - 1, z_peers[d - 1]))
    for copy in copies:
        copy.wait()
    total = z_from[0]
    for at in range(1, NZ):
        total = total + z_from[at]

    all_y[y] = total
    copies = []
    for d in range(1, NY_CHIPS):
        copies.append(
            exchange(all_y.at[y], all_y.at[y], gy_sem, d - 1, d - 1, y_peers[d - 1])
        )
    for copy in copies:
        copy.wait()

    x_slice = all_y[...].reshape(ENSEMBLE // GROUPS, COLS)
    all_x[group] = x_slice
    copies = []
    for d in range(1, GROUPS):
        there = lax.rem(group + d, GROUPS)
        copies.append(
            exchange(all_x.at[group], all_x.at[group], gx_sem, d - 1, d - 1, {"group": there})
        )
    for copy in copies:
        copy.wait()

    gram_ref[core] = all_x[...].reshape(ENSEMBLE, COLS)
    copy = exchange(gram_ref.at[core], gram_ref.at[core], gc_sem, 0, 0, partner)
    copy.wait()


STEPS = 2


def gather(state, values, precision, index):
    vmem = pl.BlockSpec(memory_space=pltpu.VMEM)
    hbm = pl.BlockSpec(memory_space=pltpu.HBM)
    dma = pltpu.SemaphoreType.DMA
    quarter = ENSEMBLE // GROUPS
    return pl.pallas_call(
        gather_kernel,
        out_shape=(
            jax.ShapeDtypeStruct((OWNERS, LOCAL, CELLS), F32),
            jax.ShapeDtypeStruct((2, ENSEMBLE, COLS), F32),
        ),
        in_specs=[hbm, hbm, vmem, vmem, vmem],
        out_specs=(vmem, vmem),
        scratch_shapes=[
            pltpu.VMEM((LOCAL * FIELDS * ROWS, COLS), F32),
            pltpu.VMEM((2, LOCAL * FIELDS, HALO, COLS), F32),
            pltpu.VMEM((OWNERS, LOCAL, CELLS), F32),
            pltpu.VMEM((2, ENSEMBLE, COLS), F32),
            pltpu.VMEM((ENSEMBLE, COLS), F32),
            pltpu.VMEM((GROUPS - 1, quarter, COLS), F32),
            pltpu.VMEM((GROUPS, quarter, COLS), F32),
            pltpu.VMEM((NY_CHIPS - 1, 8, COLS), F32),
            pltpu.VMEM((NY_CHIPS, 8, COLS), F32),
            pltpu.VMEM((NZ, 8, COLS), F32),
            pltpu.VMEM((8, COLS), F32),
            pltpu.VMEM((NY_CHIPS, 8, COLS), F32),
            pltpu.VMEM((GROUPS, quarter, COLS), F32),
            dma,
            dma((2,)),
            dma((2,)),
            dma((OWNERS,)),
            dma((OWNERS,)),
            dma((2, 1)),
            dma((2, GROUPS - 1)),
            dma((2, NY_CHIPS - 1)),
            dma((2, NZ - 1)),
            dma((2, NY_CHIPS - 1)),
            dma((2, GROUPS - 1)),
            dma((2, 1)),
        ],
        compiler_params=pltpu.CompilerParams(collective_id=0, has_side_effects=True),
        name="gather_and_gram",
    )(
        state.reshape(LOCAL * FIELDS * ROWS, COLS),
        state.reshape(LOCAL * FIELDS, ROWS // HALO, HALO, COLS),
        values,
        precision,
        index,
    )


def lane(tile, at):
    return jnp.broadcast_to(tile[:, at : at + 1], (SUB, COLS))

def sublane(tile, at):
    return jnp.broadcast_to(tile[at : at + 1, :], (SUB, COLS))

def total(terms):
    while len(terms) > 1:
        terms = [a + b for a, b in zip(terms[::2], terms[1::2])] + (
            [terms[-1]] if len(terms) % 2 else []
        )
    return terms[0]

def small_factor(tile, at):
    columns = [lane(tile, at + j) for j in range(SUB)]
    left = {(i, j): sublane(columns[j], i) for j in range(SUB) for i in range(j, SUB)}
    low, inv = {}, {}
    for j in range(SUB):
        root = lax.rsqrt(left[j, j])
        inv[j, j] = root
        for i in range(j + 1, SUB):
            low[i, j] = left[i, j] * root
        for k in range(j + 1, SUB):
            for i in range(k, SUB):
                left[i, k] = left[i, k] - low[i, j] * low[k, j]
    for j in range(SUB):
        for i in range(j + 1, SUB):
            terms = [low[i, k] * inv[k, j] for k in range(j, i)]
            inv[i, j] = -(total(terms) * inv[i, i])
    return inv

def invert_block(block, identity):
    wide = jnp.concatenate([block, identity], axis=1)
    tiles = [wide[SUB * q : SUB * (q + 1)] for q in range(BLOCK // SUB)]
    rows = lax.broadcasted_iota(jnp.int32, (SUB, COLS), 0)
    count = len(tiles)
    for p in range(count):
        inv = small_factor(tiles[p], SUB * p)
        terms = []
        for j in range(SUB):
            column = inv[SUB - 1, j]
            for i in range(SUB - 2, j - 1, -1):
                column = jnp.where(rows <= i, inv[i, j], column)
            if j > 0:
                column = jnp.where(rows < j, 0.0, column)
            terms.append(column * sublane(tiles[p], j))
        done = total(terms)
        spread = [sublane(done, k) for k in range(SUB)]
        for q in range(p + 1, count):
            source = [lane(tiles[q], SUB * p + j) for j in range(SUB)]
            terms = [
                total([inv[k, j] * source[j] for j in range(k + 1)]) * spread[k]
                for k in range(SUB)
            ]
            tiles[q] = tiles[q] - total(terms)
        tiles[p] = done
    return jnp.concatenate(tiles, axis=0)[:, BLOCK:]

def invert(work):
    n = ENSEMBLE // BLOCK
    r = lax.broadcasted_iota(jnp.int32, (BLOCK, BLOCK), 0)
    c = lax.broadcasted_iota(jnp.int32, (BLOCK, BLOCK), 1)
    identity = jnp.where(r == c, 1.0, 0.0)
    zero = jnp.zeros((BLOCK, BLOCK), F32)
    for k in range(n):
        at = k * BLOCK
        own = slice(at, at + BLOCK)
        rest = slice(at + BLOCK, ENSEMBLE)
        inverse = invert_block(work[own, own], identity)
        if k < n - 1:
            factor = dot_nt(work[rest, own], inverse)
        work[own, own] = identity
        solved = dot_nn(inverse, work[own, :])
        work[own, :] = solved
        if k < n - 1:
            work[rest, own] = jnp.zeros((ENSEMBLE - at - BLOCK, BLOCK), F32)
            work[rest, :] = work[rest, :] - dot_nn(factor, solved)

def make_transform(both_ref, work):
    r = lax.broadcasted_iota(jnp.int32, (COLS, COLS), 0)
    c = lax.broadcasted_iota(jnp.int32, (COLS, COLS), 1)
    eye = jnp.where(r == c, 1.0, 0.0)
    below = both_ref[0, COLS:, :]
    work[:COLS, :COLS] = both_ref[0, :COLS, :] + eye
    work[COLS:, :COLS] = below
    work[:COLS, COLS:] = below.T
    work[COLS:, COLS:] = both_ref[1, COLS:, :] + eye
    pull = jnp.concatenate([both_ref[1, 0:1, :], both_ref[1, 1:2, :]], axis=1)
    invert(work)
    r = lax.broadcasted_iota(jnp.int32, (ENSEMBLE, ENSEMBLE), 0)
    c = lax.broadcasted_iota(jnp.int32, (ENSEMBLE, ENSEMBLE), 1)
    inverse = jnp.where(r >= c, work[...], 0.0)
    inner = dot_nt(jnp.broadcast_to(pull, (SUB, ENSEMBLE)), inverse)
    weights = dot_nn(inner, inverse)
    return inverse + weights[0:1, :]


def return_kernel(values_ref, both_ref, out_ref, work, sendbuf, arrived, send_sem, recv_sem):
    group, member, _ = place()
    me = group * MEMBERS + member
    barrier = pltpu.get_barrier_semaphore()
    owners = list(other_owners(group, member))
    for k in owners:
        pl.semaphore_signal(barrier, inc=1, device_id=owner_id(k), device_id_type=MESH)
    transform = make_transform(both_ref, work)
    values = values_ref[...].reshape(ENSEMBLE, CELLS)
    mean = jnp.sum(values, axis=0, keepdims=True) * (1.0 / ENSEMBLE)
    updated = dot_nn(transform, values - mean) + mean
    sendbuf[...] = updated.reshape(OWNERS, LOCAL, CELLS)
    pl.semaphore_wait(barrier, OWNERS - 1)

    def copy(k, slot):
        return pltpu.make_async_remote_copy(
            src_ref=sendbuf.at[k],
            dst_ref=arrived.at[slot],
            send_sem=send_sem.at[k],
            recv_sem=recv_sem.at[slot],
            device_id=owner_id(k),
            device_id_type=MESH,
        )

    for k in owners:
        copy(k, me).start()
    arrived[me] = sendbuf[me]
    for k in owners:
        copy(k, me).wait_send()
    for k in owners:
        copy(k, k).wait_recv()
    for row in range(ROWS):
        for field in range(FIELDS):
            out_ref[pl.ds(field * ROWS + row, LOCAL, stride=FIELDS * ROWS), :] = arrived[
                row, :, field * COLS : (field + 1) * COLS
            ]


def give_back(values, both):
    vmem = pl.BlockSpec(memory_space=pltpu.VMEM)
    dma = pltpu.SemaphoreType.DMA
    out = pl.pallas_call(
        return_kernel,
        out_shape=jax.ShapeDtypeStruct((LOCAL * FIELDS * ROWS, COLS), F32),
        in_specs=[vmem, vmem],
        out_specs=vmem,
        scratch_shapes=[
            pltpu.VMEM((ENSEMBLE, ENSEMBLE), F32),
            pltpu.VMEM((OWNERS, LOCAL, CELLS), F32),
            pltpu.VMEM((OWNERS, LOCAL, CELLS), F32),
            dma((OWNERS,)),
            dma((OWNERS,)),
        ],
        compiler_params=pltpu.CompilerParams(collective_id=1, has_side_effects=True),
        name="transform_and_return",
    )(values, both)
    return out.reshape(LOCAL, FIELDS, ROWS, COLS)


def on_device(height_velocity_tensor, obs_values, obs_precision, obs_index):
    values, both = gather(height_velocity_tensor, obs_values, obs_precision, obs_index)
    return give_back(values, both)


def solution(mesh):
    return jax.shard_map(
        on_device,
        mesh=mesh,
        in_specs=(
            P(("group", "member"), None, "space", None),
            P(("group", "member", "space"), None),
            P(("group", "member", "space"), None),
            P(("group", "member", "space"), None),
        ),
        out_specs=P(("group", "member"), None, "space", None),
        check_vma=False,
    )
```

```python
import math

import jax
import jax.numpy as jnp
from jax import lax
from jax.experimental import pallas as pl
from jax.experimental.pallas import tpu as pltpu
from jax.sharding import PartitionSpec as P

GRAV = 0.4
DEPTH = 0.4
GROUPS, MEMBERS, SPACES = 4, 8, 24
NZ, NY_CHIPS = 12, 8
OWNERS = GROUPS * MEMBERS
ROWS = 32
LOCAL = 8
ENSEMBLE = OWNERS * LOCAL
FIELDS = 3
COLS = 128
CELLS = FIELDS * COLS
OBS = 192
HALO = 4
BLOCK, SUB = 64, 8
MESH = pl.DeviceIdType.MESH
F32 = jnp.float32
HIGHEST = lax.Precision.HIGHEST
SCALE = 1.0 / math.sqrt(ENSEMBLE - 1)


def dot_nt(a, b):
    return lax.dot_general(
        a, b, (((1,), (1,)), ((), ())), precision=HIGHEST, preferred_element_type=F32
    )


def dot_nn(a, b):
    return lax.dot_general(
        a, b, (((1,), (0,)), ((), ())), precision=HIGHEST, preferred_element_type=F32
    )


def place():
    group = lax.axis_index("group")
    member = lax.axis_index("member")
    space = lax.axis_index("space")
    return group, member, space


def owner_id(k):
    return {"group": k // MEMBERS, "member": lax.rem(k, MEMBERS)}


SETS = [(2, 0), (2, 1), (1, 0), (1, 1), (3, 0), (3, 1), (0, 1)]


def hops(offset):
    return min(offset[0], GROUPS - offset[0]) + 3 * min(offset[1], 4 - offset[1])


OFFSETS = sorted(
    [(a, b, c) for a in range(GROUPS) for b in range(4) for c in range(2) if a + b + c],
    key=hops,
    reverse=True,
)


def other_owners(group, member):
    z_part, core = member // 2, lax.rem(member, 2)
    for a, b, c in OFFSETS:
        there = lax.rem(group + a, GROUPS) * MEMBERS
        yield there + lax.rem(z_part + b, 4) * 2 + lax.rem(core + c, 2)


def z_id(z, core, y):
    return {"member": z // 3 * 2 + core, "space": lax.rem(z, 3) * NY_CHIPS + y}


def across_y(field):
    return pltpu.roll(field, COLS - 1, 1) - pltpu.roll(field, 1, 1)


class Forecast:
    def __init__(self, load, outside):
        self.load = load
        self.outside = outside
        self.known = {}

    def masked(self, row, value):
        flag = self.outside(row)
        return value if flag is None else jnp.where(flag, 0.0, value)

    def get(self, field, step, row):
        key = (field, step, row)
        if key not in self.known:
            self.known[key] = self.compute(field, step, row)
        return self.known[key]

    def compute(self, field, step, row):
        if step == 0:
            return self.masked(row, self.load(field, row))
        if field == 1:
            ahead, behind = self.get(0, step - 1, row + 1), self.get(0, step - 1, row - 1)
            return self.masked(row, self.get(1, step - 1, row) - GRAV * (ahead - behind))
        if field == 2:
            return self.get(2, step - 1, row) - GRAV * across_y(self.get(0, step - 1, row))
        ahead, behind = self.get(1, step, row + 1), self.get(1, step, row - 1)
        change = ahead - behind + across_y(self.get(2, step, row))
        return self.masked(row, self.get(0, step - 1, row) - DEPTH * change)


def gather_kernel(
    x_hbm_ref,
    x_halo_ref,
    value_ref,
    precision_ref,
    index_ref,
    values_ref,
    gram_ref,
    x_ref,
    halo,
    sendbuf,
    mine,
    corebuf,
    x_from,
    x_to,
    y_from,
    y_to,
    z_from,
    z_own,
    x_in_sem,
    halo_send,
    halo_recv,
    a2a_send,
    a2a_recv,
    core_sem,
    x_sem,
    y_sem,
    z_sem,
    gy_sem,
    gx_sem,
):
    group, member, space = place()
    core = lax.rem(member, 2)
    z = member // 2 * 3 + space // NY_CHIPS
    y = lax.rem(space, NY_CHIPS)
    me = group * MEMBERS + member

    x_in = pltpu.make_async_copy(x_hbm_ref, x_ref, x_in_sem)
    x_in.start()

    barrier = pltpu.get_barrier_semaphore()
    above, below = lax.rem(space + SPACES - 1, SPACES), lax.rem(space + 1, SPACES)
    peers = [{"space": above}, {"space": below}]
    owners = list(other_owners(group, member))
    peers += [owner_id(k) for k in owners]
    y_peers = [
        {"space": space - y + lax.rem(y + d, NY_CHIPS)} for d in range(1, NY_CHIPS)
    ]
    z_peers = [z_id(lax.rem(z + d, NZ), core, y) for d in range(1, NZ)]
    peers += y_peers + z_peers
    for peer in peers:
        pl.semaphore_signal(barrier, inc=1, device_id=peer, device_id_type=MESH)

    cells = lax.broadcasted_iota(jnp.int32, (CELLS, OBS), 0)
    picked = jnp.where(cells == index_ref[0:1, :], 1.0, 0.0)
    spread = dot_nt(jnp.broadcast_to(precision_ref[...], (SUB, OBS)), picked)
    weight = spread[0:1, :] * SCALE
    spread = dot_nt(jnp.broadcast_to(value_ref[...], (SUB, OBS)), picked)
    seen_value = spread[0:1, :]

    flat = [halo.at[i].reshape(LOCAL * FIELDS * HALO, COLS) for i in range(2)]

    def load(field, row):
        if row < 0:
            start = field * HALO + row + HALO
            return flat[0][pl.ds(start, LOCAL, stride=FIELDS * HALO), :]
        if row >= ROWS:
            start = field * HALO + row - ROWS
            return flat[1][pl.ds(start, LOCAL, stride=FIELDS * HALO), :]
        return x_ref[pl.ds(field * ROWS + row, LOCAL, stride=FIELDS * ROWS), :]

    first, last = space == 0, space == SPACES - 1

    def outside(row):
        return first if row < 0 else last if row >= ROWS else None

    forecast = Forecast(load, outside)

    def block_copy(k):
        return pltpu.make_async_remote_copy(
            src_ref=sendbuf.at[k],
            dst_ref=values_ref.at[me],
            send_sem=a2a_send.at[k],
            recv_sem=a2a_recv.at[me],
            device_id=owner_id(k),
            device_id_type=MESH,
        )

    def emit(rows):
        for row in rows:
            for field in range(FIELDS):
                sendbuf[row, :, field * COLS : (field + 1) * COLS] = forecast.get(
                    field, STEPS, row
                )

    x_in.wait()
    emit(range(HALO, ROWS - HALO))
    pl.semaphore_wait(barrier, len(peers))

    up = pltpu.make_async_remote_copy(
        src_ref=x_halo_ref.at[:, 0],
        dst_ref=halo.at[1],
        send_sem=halo_send.at[0],
        recv_sem=halo_recv.at[1],
        device_id={"space": above},
        device_id_type=MESH,
    )
    down = pltpu.make_async_remote_copy(
        src_ref=x_halo_ref.at[:, ROWS // HALO - 1],
        dst_ref=halo.at[0],
        send_sem=halo_send.at[1],
        recv_sem=halo_recv.at[0],
        device_id={"space": below},
        device_id_type=MESH,
    )
    up.start()
    down.start()

    def is_inner(k):
        return jnp.logical_and(k >= HALO, k < ROWS - HALO)

    for k in owners:

        @pl.when(is_inner(k))
        def _():
            block_copy(k).start()

    up.wait()
    down.wait()
    emit(list(range(HALO)) + list(range(ROWS - HALO, ROWS)))
    for k in owners:

        @pl.when(jnp.logical_not(is_inner(k)))
        def _():
            block_copy(k).start()

    values_ref[me] = sendbuf[me]
    for k in owners:
        block_copy(k).wait_send()
    for k in owners:
        pltpu.make_async_remote_copy(
            src_ref=sendbuf.at[k],
            dst_ref=values_ref.at[k],
            send_sem=a2a_send.at[k],
            recv_sem=a2a_recv.at[k],
            device_id=owner_id(k),
            device_id_type=MESH,
        ).wait_recv()

    values = values_ref[...].reshape(ENSEMBLE, CELLS)
    mean = jnp.sum(values, axis=0, keepdims=True) * (1.0 / ENSEMBLE)
    scaled = (values - mean) * weight
    innovation = weight * (seen_value - mean)
    gram = dot_nt(scaled, scaled)
    pull = dot_nt(jnp.broadcast_to(innovation, (8, CELLS)), scaled)[0:1, :]
    left, right = gram[:, :COLS], gram[:, COLS:]
    mine[0] = left
    mine[1] = right
    mine[1, 0:1, :] = pull[:, :COLS]
    mine[1, 1:2, :] = pull[:, COLS:]

    def exchange(src, dst, sem_pair, slot_send, slot_recv, device):
        copy = pltpu.make_async_remote_copy(
            src_ref=src,
            dst_ref=dst,
            send_sem=sem_pair.at[0, slot_send],
            recv_sem=sem_pair.at[1, slot_recv],
            device_id=device,
            device_id_type=MESH,
        )
        copy.start()
        return copy

    partner = {"member": member + 1 - 2 * core}
    copy = exchange(mine.at[1 - core], corebuf, core_sem, 0, 0, partner)
    copy.wait()
    half = mine[core] + corebuf[...]
    x_to[...] = half.reshape(GROUPS, ENSEMBLE // GROUPS, COLS)

    copies = []
    for d in range(1, GROUPS):
        there = lax.rem(group + d, GROUPS)
        copies.append(
            exchange(x_to.at[there], x_from.at[d - 1], x_sem, d - 1, d - 1, {"group": there})
        )
    for copy in copies:
        copy.wait()
    quarter = x_to[group] + (x_from[0] + x_from[1] + x_from[2])
    y_to[...] = quarter.reshape(NY_CHIPS, 8, COLS)

    copies = []
    for d in range(1, NY_CHIPS):
        there = lax.rem(y + d, NY_CHIPS)
        copies.append(
            exchange(y_to.at[there], y_from.at[d - 1], y_sem, d - 1, d - 1, y_peers[d - 1])
        )
    for copy in copies:
        copy.wait()
    tile = y_to[y]
    for d in range(1, NY_CHIPS):
        tile = tile + y_from[d - 1]

    z_own[...] = tile
    z_from[z] = tile
    copies = []
    for d in range(1, NZ):
        copies.append(exchange(z_own, z_from.at[z], z_sem, d - 1, d - 1, z_peers[d - 1]))
    for copy in copies:
        copy.wait()
    total = z_from[0]
    for at in range(1, NZ):
        total = total + z_from[at]

    own = gram_ref.at[core, group]
    own[y] = total
    copies = []
    for d in range(1, NY_CHIPS):
        copies.append(exchange(own.at[y], own.at[y], gy_sem, d - 1, d - 1, y_peers[d - 1]))
    for copy in copies:
        copy.wait()

    copies = []
    for slot, (step, other) in enumerate(SETS):
        there = lax.rem(group + step, GROUPS)
        device = {"group": there, "member": member + other * (1 - 2 * core)}
        copies.append(exchange(own, own, gx_sem, slot, slot, device))
    for copy in copies:
        copy.wait()


STEPS = 2


def gather(state, values, precision, index):
    vmem = pl.BlockSpec(memory_space=pltpu.VMEM)
    hbm = pl.BlockSpec(memory_space=pltpu.HBM)
    dma = pltpu.SemaphoreType.DMA
    quarter = ENSEMBLE // GROUPS
    return pl.pallas_call(
        gather_kernel,
        out_shape=(
            jax.ShapeDtypeStruct((OWNERS, LOCAL, CELLS), F32),
            jax.ShapeDtypeStruct((2, GROUPS, NY_CHIPS, 8, COLS), F32),
        ),
        in_specs=[hbm, hbm, vmem, vmem, vmem],
        out_specs=(vmem, vmem),
        scratch_shapes=[
            pltpu.VMEM((LOCAL * FIELDS * ROWS, COLS), F32),
            pltpu.VMEM((2, LOCAL * FIELDS, HALO, COLS), F32),
            pltpu.VMEM((OWNERS, LOCAL, CELLS), F32),
            pltpu.VMEM((2, ENSEMBLE, COLS), F32),
            pltpu.VMEM((ENSEMBLE, COLS), F32),
            pltpu.VMEM((GROUPS - 1, quarter, COLS), F32),
            pltpu.VMEM((GROUPS, quarter, COLS), F32),
            pltpu.VMEM((NY_CHIPS - 1, 8, COLS), F32),
            pltpu.VMEM((NY_CHIPS, 8, COLS), F32),
            pltpu.VMEM((NZ, 8, COLS), F32),
            pltpu.VMEM((8, COLS), F32),
            dma,
            dma((2,)),
            dma((2,)),
            dma((OWNERS,)),
            dma((OWNERS,)),
            dma((2, 1)),
            dma((2, GROUPS - 1)),
            dma((2, NY_CHIPS - 1)),
            dma((2, NZ - 1)),
            dma((2, NY_CHIPS - 1)),
            dma((2, len(SETS))),
        ],
        compiler_params=pltpu.CompilerParams(collective_id=0, has_side_effects=True),
        name="gather_and_gram",
    )(
        state.reshape(LOCAL * FIELDS * ROWS, COLS),
        state.reshape(LOCAL * FIELDS, ROWS // HALO, HALO, COLS),
        values,
        precision,
        index,
    )


def lane(tile, at):
    return jnp.broadcast_to(tile[:, at : at + 1], (SUB, COLS))

def sublane(tile, at):
    return jnp.broadcast_to(tile[at : at + 1, :], (SUB, COLS))

def total(terms):
    while len(terms) > 1:
        terms = [a + b for a, b in zip(terms[::2], terms[1::2])] + (
            [terms[-1]] if len(terms) % 2 else []
        )
    return terms[0]

def small_factor(tile, at):
    columns = [lane(tile, at + j) for j in range(SUB)]
    left = {(i, j): sublane(columns[j], i) for j in range(SUB) for i in range(j, SUB)}
    low, inv = {}, {}
    for j in range(0, SUB, 2):
        n = j + 1
        first, cross, second = left[j, j], left[n, j], left[n, n]
        root = lax.rsqrt(first)
        root_pair = lax.rsqrt(first * second - cross * cross)
        inv[j, j] = root
        inv[n, n] = root_pair * (first * root)
        for i in range(n, SUB):
            low[i, j] = left[i, j] * root
        for i in range(n + 1, SUB):
            low[i, n] = (left[i, n] - low[i, j] * low[n, j]) * inv[n, n]
        for k in range(n + 1, SUB):
            for i in range(k, SUB):
                left[i, k] = left[i, k] - low[i, j] * low[k, j] - low[i, n] * low[k, n]
    for j in range(SUB):
        for i in range(j + 1, SUB):
            terms = [low[i, k] * inv[k, j] for k in range(j, i)]
            inv[i, j] = -(total(terms) * inv[i, i])
    return inv

def invert_block(block, identity):
    wide = jnp.concatenate([block, identity], axis=1)
    tiles = [wide[SUB * q : SUB * (q + 1)] for q in range(BLOCK // SUB)]
    rows = lax.broadcasted_iota(jnp.int32, (SUB, COLS), 0)
    count = len(tiles)
    for p in range(count):
        inv = small_factor(tiles[p], SUB * p)
        terms = []
        for j in range(SUB):
            column = inv[SUB - 1, j]
            for i in range(SUB - 2, j - 1, -1):
                column = jnp.where(rows <= i, inv[i, j], column)
            if j > 0:
                column = jnp.where(rows < j, 0.0, column)
            terms.append(column * sublane(tiles[p], j))
        done = total(terms)
        spread = [sublane(done, k) for k in range(SUB)]
        for q in range(p + 1, count):
            source = [lane(tiles[q], SUB * p + j) for j in range(SUB)]
            terms = [
                total([inv[k, j] * source[j] for j in range(k + 1)]) * spread[k]
                for k in range(SUB)
            ]
            tiles[q] = tiles[q] - total(terms)
        tiles[p] = done
    return jnp.concatenate(tiles, axis=0)[:, BLOCK:]

def invert(work):
    n = ENSEMBLE // BLOCK
    r = lax.broadcasted_iota(jnp.int32, (BLOCK, BLOCK), 0)
    c = lax.broadcasted_iota(jnp.int32, (BLOCK, BLOCK), 1)
    identity = jnp.where(r == c, 1.0, 0.0)
    zero = jnp.zeros((BLOCK, BLOCK), F32)
    for k in range(n):
        at = k * BLOCK
        own = slice(at, at + BLOCK)
        rest = slice(at + BLOCK, ENSEMBLE)
        inverse = invert_block(work[own, own], identity)
        if k < n - 1:
            factor = dot_nt(work[rest, own], inverse)
        work[own, own] = identity
        solved = dot_nn(inverse, work[own, :])
        work[own, :] = solved
        if k < n - 1:
            work[rest, own] = jnp.zeros((ENSEMBLE - at - BLOCK, BLOCK), F32)
            work[rest, :] = work[rest, :] - dot_nn(factor, solved)

def make_transform(both_ref, work):
    r = lax.broadcasted_iota(jnp.int32, (COLS, COLS), 0)
    c = lax.broadcasted_iota(jnp.int32, (COLS, COLS), 1)
    eye = jnp.where(r == c, 1.0, 0.0)
    left = both_ref[0].reshape(ENSEMBLE, COLS)
    right = both_ref[1].reshape(ENSEMBLE, COLS)
    work[:COLS, :COLS] = left[:COLS] + eye
    work[COLS:, :COLS] = left[COLS:]
    work[:COLS, COLS:] = left[COLS:].T
    work[COLS:, COLS:] = right[COLS:] + eye
    pull = jnp.concatenate([right[0:1], right[1:2]], axis=1)
    invert(work)
    r = lax.broadcasted_iota(jnp.int32, (ENSEMBLE, ENSEMBLE), 0)
    c = lax.broadcasted_iota(jnp.int32, (ENSEMBLE, ENSEMBLE), 1)
    inverse = jnp.where(r >= c, work[...], 0.0)
    inner = dot_nt(jnp.broadcast_to(pull, (SUB, ENSEMBLE)), inverse)
    weights = dot_nn(inner, inverse)
    return inverse + weights[0:1, :]


def return_kernel(values_ref, both_ref, out_ref, work, sendbuf, arrived, send_sem, recv_sem):
    group, member, _ = place()
    me = group * MEMBERS + member
    barrier = pltpu.get_barrier_semaphore()
    owners = list(other_owners(group, member))
    for k in owners:
        pl.semaphore_signal(barrier, inc=1, device_id=owner_id(k), device_id_type=MESH)
    transform = make_transform(both_ref, work)
    values = values_ref[...].reshape(ENSEMBLE, CELLS)
    mean = jnp.sum(values, axis=0, keepdims=True) * (1.0 / ENSEMBLE)
    updated = dot_nn(transform, values - mean) + mean
    sendbuf[...] = updated.reshape(OWNERS, LOCAL, CELLS)
    pl.semaphore_wait(barrier, OWNERS - 1)

    def copy(k, slot):
        return pltpu.make_async_remote_copy(
            src_ref=sendbuf.at[k],
            dst_ref=arrived.at[slot],
            send_sem=send_sem.at[k],
            recv_sem=recv_sem.at[slot],
            device_id=owner_id(k),
            device_id_type=MESH,
        )

    for k in owners:
        copy(k, me).start()
    arrived[me] = sendbuf[me]
    for k in owners:
        copy(k, me).wait_send()
    for k in owners:
        copy(k, k).wait_recv()
    for row in range(ROWS):
        for field in range(FIELDS):
            out_ref[pl.ds(field * ROWS + row, LOCAL, stride=FIELDS * ROWS), :] = arrived[
                row, :, field * COLS : (field + 1) * COLS
            ]


def give_back(values, both):
    vmem = pl.BlockSpec(memory_space=pltpu.VMEM)
    dma = pltpu.SemaphoreType.DMA
    out = pl.pallas_call(
        return_kernel,
        out_shape=jax.ShapeDtypeStruct((LOCAL * FIELDS * ROWS, COLS), F32),
        in_specs=[vmem, vmem],
        out_specs=vmem,
        scratch_shapes=[
            pltpu.VMEM((ENSEMBLE, ENSEMBLE), F32),
            pltpu.VMEM((OWNERS, LOCAL, CELLS), F32),
            pltpu.VMEM((OWNERS, LOCAL, CELLS), F32),
            dma((OWNERS,)),
            dma((OWNERS,)),
        ],
        compiler_params=pltpu.CompilerParams(collective_id=1, has_side_effects=True),
        name="transform_and_return",
    )(values, both)
    return out.reshape(LOCAL, FIELDS, ROWS, COLS)


def on_device(height_velocity_tensor, obs_values, obs_precision, obs_index):
    values, both = gather(height_velocity_tensor, obs_values, obs_precision, obs_index)
    return give_back(values, both)


def solution(mesh):
    return jax.shard_map(
        on_device,
        mesh=mesh,
        in_specs=(
            P(("group", "member"), None, "space", None),
            P(("group", "member", "space"), None),
            P(("group", "member", "space"), None),
            P(("group", "member", "space"), None),
        ),
        out_specs=P(("group", "member"), None, "space", None),
        check_vma=False,
    )
```

```python
import math

import jax
import jax.numpy as jnp
from jax import lax
from jax.experimental import pallas as pl
from jax.experimental.pallas import tpu as pltpu
from jax.sharding import PartitionSpec as P

GRAV = 0.4
DEPTH = 0.4
GROUPS, MEMBERS, SPACES = 4, 8, 24
NZ, NY_CHIPS = 12, 8
OWNERS = GROUPS * MEMBERS
ROWS = 32
LOCAL = 8
ENSEMBLE = OWNERS * LOCAL
FIELDS = 3
COLS = 128
CELLS = FIELDS * COLS
OBS = 192
HALO = 4
BLOCK, SUB = 64, 8
MESH = pl.DeviceIdType.MESH
F32 = jnp.float32
HIGHEST = lax.Precision.HIGHEST
SCALE = 1.0 / math.sqrt(ENSEMBLE - 1)


def dot_nt(a, b):
    return lax.dot_general(
        a, b, (((1,), (1,)), ((), ())), precision=HIGHEST, preferred_element_type=F32
    )


def dot_nn(a, b):
    return lax.dot_general(
        a, b, (((1,), (0,)), ((), ())), precision=HIGHEST, preferred_element_type=F32
    )


def place():
    group = lax.axis_index("group")
    member = lax.axis_index("member")
    space = lax.axis_index("space")
    return group, member, space


def owner_id(k):
    return {"group": k // MEMBERS, "member": lax.rem(k, MEMBERS)}


SETS = [(2, 0), (2, 1), (1, 0), (1, 1), (3, 0), (3, 1), (0, 1)]


def hops(offset):
    return min(offset[0], GROUPS - offset[0]) + 3 * min(offset[1], 4 - offset[1])


OFFSETS = sorted(
    [(a, b, c) for a in range(GROUPS) for b in range(4) for c in range(2) if a + b + c],
    key=hops,
    reverse=True,
)


def other_owners(group, member):
    z_part, core = member // 2, lax.rem(member, 2)
    for a, b, c in OFFSETS:
        there = lax.rem(group + a, GROUPS) * MEMBERS
        yield there + lax.rem(z_part + b, 4) * 2 + lax.rem(core + c, 2)


def z_id(z, core, y):
    return {"member": z // 3 * 2 + core, "space": lax.rem(z, 3) * NY_CHIPS + y}


def across_y(field):
    return pltpu.roll(field, COLS - 1, 1) - pltpu.roll(field, 1, 1)


class Forecast:
    def __init__(self, load, outside):
        self.load = load
        self.outside = outside
        self.known = {}

    def masked(self, row, value):
        flag = self.outside(row)
        return value if flag is None else jnp.where(flag, 0.0, value)

    def get(self, field, step, row):
        key = (field, step, row)
        if key not in self.known:
            self.known[key] = self.compute(field, step, row)
        return self.known[key]

    def compute(self, field, step, row):
        if step == 0:
            return self.masked(row, self.load(field, row))
        if field == 1:
            ahead, behind = self.get(0, step - 1, row + 1), self.get(0, step - 1, row - 1)
            return self.masked(row, self.get(1, step - 1, row) - GRAV * (ahead - behind))
        if field == 2:
            return self.get(2, step - 1, row) - GRAV * across_y(self.get(0, step - 1, row))
        ahead, behind = self.get(1, step, row + 1), self.get(1, step, row - 1)
        change = ahead - behind + across_y(self.get(2, step, row))
        return self.masked(row, self.get(0, step - 1, row) - DEPTH * change)


def gather_kernel(
    x_hbm_ref,
    x_halo_ref,
    value_ref,
    precision_ref,
    index_ref,
    values_ref,
    gram_ref,
    x_ref,
    halo,
    sendbuf,
    mine,
    corebuf,
    x_from,
    x_to,
    y_from,
    y_to,
    z_from,
    z_own,
    x_in_sem,
    halo_send,
    halo_recv,
    a2a_send,
    a2a_recv,
    core_sem,
    x_sem,
    y_sem,
    z_sem,
    gy_sem,
    gx_sem,
):
    group, member, space = place()
    core = lax.rem(member, 2)
    z = member // 2 * 3 + space // NY_CHIPS
    y = lax.rem(space, NY_CHIPS)
    me = group * MEMBERS + member

    x_in = pltpu.make_async_copy(x_hbm_ref, x_ref, x_in_sem)
    x_in.start()

    barrier = pltpu.get_barrier_semaphore()
    above, below = lax.rem(space + SPACES - 1, SPACES), lax.rem(space + 1, SPACES)
    peers = [{"space": above}, {"space": below}]
    owners = list(other_owners(group, member))
    peers += [owner_id(k) for k in owners]
    y_peers = [
        {"space": space - y + lax.rem(y + d, NY_CHIPS)} for d in range(1, NY_CHIPS)
    ]
    z_peers = [z_id(lax.rem(z + d, NZ), core, y) for d in range(1, NZ)]
    peers += y_peers + z_peers
    for peer in peers:
        pl.semaphore_signal(barrier, inc=1, device_id=peer, device_id_type=MESH)

    cells = lax.broadcasted_iota(jnp.int32, (CELLS, OBS), 0)
    picked = jnp.where(cells == index_ref[0:1, :], 1.0, 0.0)
    spread = dot_nt(jnp.broadcast_to(precision_ref[...], (SUB, OBS)), picked)
    weight = spread[0:1, :] * SCALE
    spread = dot_nt(jnp.broadcast_to(value_ref[...], (SUB, OBS)), picked)
    seen_value = spread[0:1, :]

    flat = [halo.at[i].reshape(LOCAL * FIELDS * HALO, COLS) for i in range(2)]

    def load(field, row):
        if row < 0:
            start = field * HALO + row + HALO
            return flat[0][pl.ds(start, LOCAL, stride=FIELDS * HALO), :]
        if row >= ROWS:
            start = field * HALO + row - ROWS
            return flat[1][pl.ds(start, LOCAL, stride=FIELDS * HALO), :]
        return x_ref[pl.ds(field * ROWS + row, LOCAL, stride=FIELDS * ROWS), :]

    first, last = space == 0, space == SPACES - 1

    def outside(row):
        return first if row < 0 else last if row >= ROWS else None

    forecast = Forecast(load, outside)

    def block_copy(k):
        return pltpu.make_async_remote_copy(
            src_ref=sendbuf.at[k],
            dst_ref=values_ref.at[me],
            send_sem=a2a_send.at[k],
            recv_sem=a2a_recv.at[me],
            device_id=owner_id(k),
            device_id_type=MESH,
        )

    def emit(rows):
        for row in rows:
            for field in range(FIELDS):
                sendbuf[row, :, field * COLS : (field + 1) * COLS] = forecast.get(
                    field, STEPS, row
                )

    x_in.wait()
    emit(range(HALO, ROWS - HALO))
    pl.semaphore_wait(barrier, len(peers))

    up = pltpu.make_async_remote_copy(
        src_ref=x_halo_ref.at[:, 0],
        dst_ref=halo.at[1],
        send_sem=halo_send.at[0],
        recv_sem=halo_recv.at[1],
        device_id={"space": above},
        device_id_type=MESH,
    )
    down = pltpu.make_async_remote_copy(
        src_ref=x_halo_ref.at[:, ROWS // HALO - 1],
        dst_ref=halo.at[0],
        send_sem=halo_send.at[1],
        recv_sem=halo_recv.at[0],
        device_id={"space": below},
        device_id_type=MESH,
    )
    up.start()
    down.start()

    def is_inner(k):
        return jnp.logical_and(k >= HALO, k < ROWS - HALO)

    for k in owners:

        @pl.when(is_inner(k))
        def _():
            block_copy(k).start()

    up.wait()
    down.wait()
    emit(list(range(HALO)) + list(range(ROWS - HALO, ROWS)))
    for k in owners:

        @pl.when(jnp.logical_not(is_inner(k)))
        def _():
            block_copy(k).start()

    values_ref[me] = sendbuf[me]
    for k in owners:
        block_copy(k).wait_send()
    for k in owners:
        pltpu.make_async_remote_copy(
            src_ref=sendbuf.at[k],
            dst_ref=values_ref.at[k],
            send_sem=a2a_send.at[k],
            recv_sem=a2a_recv.at[k],
            device_id=owner_id(k),
            device_id_type=MESH,
        ).wait_recv()

    values = values_ref[...].reshape(ENSEMBLE, CELLS)
    mean = jnp.sum(values, axis=0, keepdims=True) * (1.0 / ENSEMBLE)
    scaled = (values - mean) * weight
    innovation = weight * (seen_value - mean)
    gram = dot_nt(scaled, scaled)
    pull = dot_nt(jnp.broadcast_to(innovation, (8, CELLS)), scaled)[0:1, :]
    left, right = gram[:, :COLS], gram[:, COLS:]
    mine[0] = left
    mine[1] = right
    mine[1, 0:1, :] = pull[:, :COLS]
    mine[1, 1:2, :] = pull[:, COLS:]

    def exchange(src, dst, sem_pair, slot_send, slot_recv, device):
        copy = pltpu.make_async_remote_copy(
            src_ref=src,
            dst_ref=dst,
            send_sem=sem_pair.at[0, slot_send],
            recv_sem=sem_pair.at[1, slot_recv],
            device_id=device,
            device_id_type=MESH,
        )
        copy.start()
        return copy

    partner = {"member": member + 1 - 2 * core}
    copy = exchange(mine.at[1 - core], corebuf, core_sem, 0, 0, partner)
    copy.wait()
    half = mine[core] + corebuf[...]
    x_to[...] = half.reshape(GROUPS, ENSEMBLE // GROUPS, COLS)

    copies = []
    for d in range(1, GROUPS):
        there = lax.rem(group + d, GROUPS)
        copies.append(
            exchange(x_to.at[there], x_from.at[d - 1], x_sem, d - 1, d - 1, {"group": there})
        )
    for copy in copies:
        copy.wait()
    quarter = x_to[group] + (x_from[0] + x_from[1] + x_from[2])
    y_to[...] = quarter.reshape(NY_CHIPS, 8, COLS)

    copies = []
    for d in range(1, NY_CHIPS):
        there = lax.rem(y + d, NY_CHIPS)
        copies.append(
            exchange(y_to.at[there], y_from.at[d - 1], y_sem, d - 1, d - 1, y_peers[d - 1])
        )
    for copy in copies:
        copy.wait()
    tile = y_to[y]
    for d in range(1, NY_CHIPS):
        tile = tile + y_from[d - 1]

    z_own[...] = tile
    z_from[z] = tile
    copies = []
    for d in range(1, NZ):
        copies.append(exchange(z_own, z_from.at[z], z_sem, d - 1, d - 1, z_peers[d - 1]))
    for copy in copies:
        copy.wait()
    total = z_from[0]
    for at in range(1, NZ):
        total = total + z_from[at]

    own = gram_ref.at[core, group]
    own[y] = total
    copies = []
    for d in range(1, NY_CHIPS):
        copies.append(exchange(own.at[y], own.at[y], gy_sem, d - 1, d - 1, y_peers[d - 1]))
    for copy in copies:
        copy.wait()

    copies = []
    for slot, (step, other) in enumerate(SETS):
        there = lax.rem(group + step, GROUPS)
        device = {"group": there, "member": member + other * (1 - 2 * core)}
        copies.append(exchange(own, own, gx_sem, slot, slot, device))
    for copy in copies:
        copy.wait()


STEPS = 2


def gather(state, values, precision, index):
    vmem = pl.BlockSpec(memory_space=pltpu.VMEM)
    hbm = pl.BlockSpec(memory_space=pltpu.HBM)
    dma = pltpu.SemaphoreType.DMA
    quarter = ENSEMBLE // GROUPS
    return pl.pallas_call(
        gather_kernel,
        out_shape=(
            jax.ShapeDtypeStruct((OWNERS, LOCAL, CELLS), F32),
            jax.ShapeDtypeStruct((2, GROUPS, NY_CHIPS, 8, COLS), F32),
        ),
        in_specs=[hbm, hbm, vmem, vmem, vmem],
        out_specs=(vmem, vmem),
        scratch_shapes=[
            pltpu.VMEM((LOCAL * FIELDS * ROWS, COLS), F32),
            pltpu.VMEM((2, LOCAL * FIELDS, HALO, COLS), F32),
            pltpu.VMEM((OWNERS, LOCAL, CELLS), F32),
            pltpu.VMEM((2, ENSEMBLE, COLS), F32),
            pltpu.VMEM((ENSEMBLE, COLS), F32),
            pltpu.VMEM((GROUPS - 1, quarter, COLS), F32),
            pltpu.VMEM((GROUPS, quarter, COLS), F32),
            pltpu.VMEM((NY_CHIPS - 1, 8, COLS), F32),
            pltpu.VMEM((NY_CHIPS, 8, COLS), F32),
            pltpu.VMEM((NZ, 8, COLS), F32),
            pltpu.VMEM((8, COLS), F32),
            dma,
            dma((2,)),
            dma((2,)),
            dma((OWNERS,)),
            dma((OWNERS,)),
            dma((2, 1)),
            dma((2, GROUPS - 1)),
            dma((2, NY_CHIPS - 1)),
            dma((2, NZ - 1)),
            dma((2, NY_CHIPS - 1)),
            dma((2, len(SETS))),
        ],
        compiler_params=pltpu.CompilerParams(collective_id=0, has_side_effects=True),
        name="gather_and_gram",
    )(
        state.reshape(LOCAL * FIELDS * ROWS, COLS),
        state.reshape(LOCAL * FIELDS, ROWS // HALO, HALO, COLS),
        values,
        precision,
        index,
    )


def lane(tile, at):
    return jnp.broadcast_to(tile[:, at : at + 1], (SUB, COLS))

def sublane(tile, at):
    return jnp.broadcast_to(tile[at : at + 1, :], (SUB, COLS))

def total(terms):
    while len(terms) > 1:
        terms = [a + b for a, b in zip(terms[::2], terms[1::2])] + (
            [terms[-1]] if len(terms) % 2 else []
        )
    return terms[0]

def small_factor(columns):
    left = {(i, j): sublane(columns[j], i) for j in range(SUB) for i in range(j, SUB)}
    low, inv = {}, {}
    for j in range(0, SUB, 2):
        n = j + 1
        first, cross, second = left[j, j], left[n, j], left[n, n]
        root = lax.rsqrt(first)
        root_pair = lax.rsqrt(first * second - cross * cross)
        inv[j, j] = root
        inv[n, n] = root_pair * (first * root)
        for i in range(n, SUB):
            low[i, j] = left[i, j] * root
        for i in range(n + 1, SUB):
            low[i, n] = (left[i, n] - low[i, j] * low[n, j]) * inv[n, n]
        for k in range(n + 1, SUB):
            for i in range(k, SUB):
                left[i, k] = left[i, k] - low[i, j] * low[k, j] - low[i, n] * low[k, n]
    for j in range(SUB):
        for i in range(j + 1, SUB):
            terms = [low[i, k] * inv[k, j] for k in range(j, i)]
            inv[i, j] = -(total(terms) * inv[i, i])
    return inv

def invert_block(block, identity):
    wide = jnp.concatenate([block, identity], axis=1)
    tiles = [wide[SUB * q : SUB * (q + 1)] for q in range(BLOCK // SUB)]
    rows = lax.broadcasted_iota(jnp.int32, (SUB, COLS), 0)
    count = len(tiles)
    columns = [lane(tiles[0], j) for j in range(SUB)]
    for p in range(count):
        inv = small_factor(columns)
        terms = []
        for j in range(SUB):
            column = inv[SUB - 1, j]
            for i in range(SUB - 2, j - 1, -1):
                column = jnp.where(rows <= i, inv[i, j], column)
            if j > 0:
                column = jnp.where(rows < j, 0.0, column)
            terms.append(column * sublane(tiles[p], j))
        done = total(terms)
        spread = [sublane(done, k) for k in range(SUB)]
        for q in range(p + 1, count):
            source = [lane(tiles[q], SUB * p + j) for j in range(SUB)]
            low = [total([inv[k, j] * source[j] for j in range(k + 1)]) for k in range(SUB)]
            if q == p + 1:
                columns = [
                    lane(tiles[q], SUB * q + j)
                    - total([low[k] * sublane(low[k], j) for k in range(SUB)])
                    for j in range(SUB)
                ]
            tiles[q] = tiles[q] - total([low[k] * spread[k] for k in range(SUB)])
        tiles[p] = done
    return jnp.concatenate(tiles, axis=0)[:, BLOCK:]

def invert(work):
    n = ENSEMBLE // BLOCK
    r = lax.broadcasted_iota(jnp.int32, (BLOCK, BLOCK), 0)
    c = lax.broadcasted_iota(jnp.int32, (BLOCK, BLOCK), 1)
    identity = jnp.where(r == c, 1.0, 0.0)
    zero = jnp.zeros((BLOCK, BLOCK), F32)
    for k in range(n):
        at = k * BLOCK
        own = slice(at, at + BLOCK)
        rest = slice(at + BLOCK, ENSEMBLE)
        inverse = invert_block(work[own, own], identity)
        if k < n - 1:
            factor = dot_nt(work[rest, own], inverse)
        work[own, own] = identity
        solved = dot_nn(inverse, work[own, :])
        work[own, :] = solved
        if k < n - 1:
            work[rest, own] = jnp.zeros((ENSEMBLE - at - BLOCK, BLOCK), F32)
            work[rest, :] = work[rest, :] - dot_nn(factor, solved)

def make_transform(both_ref, work):
    r = lax.broadcasted_iota(jnp.int32, (COLS, COLS), 0)
    c = lax.broadcasted_iota(jnp.int32, (COLS, COLS), 1)
    eye = jnp.where(r == c, 1.0, 0.0)
    left = both_ref[0].reshape(ENSEMBLE, COLS)
    right = both_ref[1].reshape(ENSEMBLE, COLS)
    work[:COLS, :COLS] = left[:COLS] + eye
    work[COLS:, :COLS] = left[COLS:]
    work[:COLS, COLS:] = left[COLS:].T
    work[COLS:, COLS:] = right[COLS:] + eye
    pull = jnp.concatenate([right[0:1], right[1:2]], axis=1)
    invert(work)
    r = lax.broadcasted_iota(jnp.int32, (ENSEMBLE, ENSEMBLE), 0)
    c = lax.broadcasted_iota(jnp.int32, (ENSEMBLE, ENSEMBLE), 1)
    inverse = jnp.where(r >= c, work[...], 0.0)
    inner = dot_nt(jnp.broadcast_to(pull, (SUB, ENSEMBLE)), inverse)
    weights = dot_nn(inner, inverse)
    return inverse + weights[0:1, :]


def return_kernel(values_ref, both_ref, out_ref, work, sendbuf, arrived, send_sem, recv_sem):
    group, member, _ = place()
    me = group * MEMBERS + member
    barrier = pltpu.get_barrier_semaphore()
    owners = list(other_owners(group, member))
    for k in owners:
        pl.semaphore_signal(barrier, inc=1, device_id=owner_id(k), device_id_type=MESH)
    transform = make_transform(both_ref, work)
    values = values_ref[...].reshape(ENSEMBLE, CELLS)
    mean = jnp.sum(values, axis=0, keepdims=True) * (1.0 / ENSEMBLE)
    updated = dot_nn(transform, values - mean) + mean
    sendbuf[...] = updated.reshape(OWNERS, LOCAL, CELLS)
    pl.semaphore_wait(barrier, OWNERS - 1)

    def copy(k, slot):
        return pltpu.make_async_remote_copy(
            src_ref=sendbuf.at[k],
            dst_ref=arrived.at[slot],
            send_sem=send_sem.at[k],
            recv_sem=recv_sem.at[slot],
            device_id=owner_id(k),
            device_id_type=MESH,
        )

    for k in owners:
        copy(k, me).start()
    arrived[me] = sendbuf[me]
    for k in owners:
        copy(k, me).wait_send()
    for k in owners:
        copy(k, k).wait_recv()
    for row in range(ROWS):
        for field in range(FIELDS):
            out_ref[pl.ds(field * ROWS + row, LOCAL, stride=FIELDS * ROWS), :] = arrived[
                row, :, field * COLS : (field + 1) * COLS
            ]


def give_back(values, both):
    vmem = pl.BlockSpec(memory_space=pltpu.VMEM)
    dma = pltpu.SemaphoreType.DMA
    out = pl.pallas_call(
        return_kernel,
        out_shape=jax.ShapeDtypeStruct((LOCAL * FIELDS * ROWS, COLS), F32),
        in_specs=[vmem, vmem],
        out_specs=vmem,
        scratch_shapes=[
            pltpu.VMEM((ENSEMBLE, ENSEMBLE), F32),
            pltpu.VMEM((OWNERS, LOCAL, CELLS), F32),
            pltpu.VMEM((OWNERS, LOCAL, CELLS), F32),
            dma((OWNERS,)),
            dma((OWNERS,)),
        ],
        compiler_params=pltpu.CompilerParams(collective_id=1, has_side_effects=True),
        name="transform_and_return",
    )(values, both)
    return out.reshape(LOCAL, FIELDS, ROWS, COLS)


def on_device(height_velocity_tensor, obs_values, obs_precision, obs_index):
    values, both = gather(height_velocity_tensor, obs_values, obs_precision, obs_index)
    return give_back(values, both)


def solution(mesh):
    return jax.shard_map(
        on_device,
        mesh=mesh,
        in_specs=(
            P(("group", "member"), None, "space", None),
            P(("group", "member", "space"), None),
            P(("group", "member", "space"), None),
            P(("group", "member", "space"), None),
        ),
        out_specs=P(("group", "member"), None, "space", None),
        check_vma=False,
    )
```

```python
import math

import jax
import jax.numpy as jnp
from jax import lax
from jax.experimental import pallas as pl
from jax.experimental.pallas import tpu as pltpu
from jax.sharding import PartitionSpec as P

GRAV = 0.4
DEPTH = 0.4
GROUPS, MEMBERS, SPACES = 4, 8, 24
NZ, NY_CHIPS = 12, 8
OWNERS = GROUPS * MEMBERS
ROWS = 32
LOCAL = 8
ENSEMBLE = OWNERS * LOCAL
FIELDS = 3
COLS = 128
CELLS = FIELDS * COLS
OBS = 192
HALO = 4
BLOCK, SUB = 64, 8
MESH = pl.DeviceIdType.MESH
F32 = jnp.float32
HIGHEST = lax.Precision.HIGHEST
SCALE = 1.0 / math.sqrt(ENSEMBLE - 1)


def dot_nt(a, b):
    return lax.dot_general(
        a, b, (((1,), (1,)), ((), ())), precision=HIGHEST, preferred_element_type=F32
    )


def dot_nn(a, b):
    return lax.dot_general(
        a, b, (((1,), (0,)), ((), ())), precision=HIGHEST, preferred_element_type=F32
    )


def place():
    group = lax.axis_index("group")
    member = lax.axis_index("member")
    space = lax.axis_index("space")
    return group, member, space


def owner_id(k):
    return {"group": k // MEMBERS, "member": lax.rem(k, MEMBERS)}


SETS = [(2, 0), (2, 1), (1, 0), (1, 1), (3, 0), (3, 1), (0, 1)]


def hops(offset):
    return min(offset[0], GROUPS - offset[0]) + 3 * min(offset[1], 4 - offset[1])


OFFSETS = sorted(
    [(a, b, c) for a in range(GROUPS) for b in range(4) for c in range(2) if a + b + c],
    key=hops,
    reverse=True,
)


def other_owners(group, member):
    z_part, core = member // 2, lax.rem(member, 2)
    for a, b, c in OFFSETS:
        there = lax.rem(group + a, GROUPS) * MEMBERS
        yield there + lax.rem(z_part + b, 4) * 2 + lax.rem(core + c, 2)


def z_id(z, core, y):
    return {"member": z // 3 * 2 + core, "space": lax.rem(z, 3) * NY_CHIPS + y}


def across_y(field):
    return pltpu.roll(field, COLS - 1, 1) - pltpu.roll(field, 1, 1)


class Forecast:
    def __init__(self, load, outside):
        self.load = load
        self.outside = outside
        self.known = {}

    def masked(self, row, value):
        flag = self.outside(row)
        return value if flag is None else jnp.where(flag, 0.0, value)

    def get(self, field, step, row):
        key = (field, step, row)
        if key not in self.known:
            self.known[key] = self.compute(field, step, row)
        return self.known[key]

    def compute(self, field, step, row):
        if step == 0:
            return self.masked(row, self.load(field, row))
        if field == 1:
            ahead, behind = self.get(0, step - 1, row + 1), self.get(0, step - 1, row - 1)
            return self.masked(row, self.get(1, step - 1, row) - GRAV * (ahead - behind))
        if field == 2:
            return self.get(2, step - 1, row) - GRAV * across_y(self.get(0, step - 1, row))
        ahead, behind = self.get(1, step, row + 1), self.get(1, step, row - 1)
        change = ahead - behind + across_y(self.get(2, step, row))
        return self.masked(row, self.get(0, step - 1, row) - DEPTH * change)


def gather_kernel(
    x_hbm_ref,
    x_halo_ref,
    value_ref,
    precision_ref,
    index_ref,
    values_ref,
    gram_ref,
    x_ref,
    halo,
    sendbuf,
    mine,
    corebuf,
    x_from,
    x_to,
    y_from,
    y_to,
    z_from,
    z_own,
    x_in_sem,
    halo_send,
    halo_recv,
    a2a_send,
    a2a_recv,
    core_sem,
    x_sem,
    y_sem,
    z_sem,
    gy_sem,
    gx_sem,
):
    group, member, space = place()
    core = lax.rem(member, 2)
    z = member // 2 * 3 + space // NY_CHIPS
    y = lax.rem(space, NY_CHIPS)
    me = group * MEMBERS + member

    x_in = pltpu.make_async_copy(x_hbm_ref, x_ref, x_in_sem)
    x_in.start()

    barrier = pltpu.get_barrier_semaphore()
    above, below = lax.rem(space + SPACES - 1, SPACES), lax.rem(space + 1, SPACES)
    peers = [{"space": above}, {"space": below}]
    owners = list(other_owners(group, member))
    peers += [owner_id(k) for k in owners]
    y_peers = [
        {"space": space - y + lax.rem(y + d, NY_CHIPS)} for d in range(1, NY_CHIPS)
    ]
    z_peers = [z_id(lax.rem(z + d, NZ), core, y) for d in range(1, NZ)]
    peers += y_peers + z_peers
    for peer in peers:
        pl.semaphore_signal(barrier, inc=1, device_id=peer, device_id_type=MESH)

    cells = lax.broadcasted_iota(jnp.int32, (CELLS, OBS), 0)
    picked = jnp.where(cells == index_ref[0:1, :], 1.0, 0.0)
    spread = dot_nt(jnp.broadcast_to(precision_ref[...], (SUB, OBS)), picked)
    weight = spread[0:1, :] * SCALE
    spread = dot_nt(jnp.broadcast_to(value_ref[...], (SUB, OBS)), picked)
    seen_value = spread[0:1, :]

    flat = [halo.at[i].reshape(LOCAL * FIELDS * HALO, COLS) for i in range(2)]

    def load(field, row):
        if row < 0:
            start = field * HALO + row + HALO
            return flat[0][pl.ds(start, LOCAL, stride=FIELDS * HALO), :]
        if row >= ROWS:
            start = field * HALO + row - ROWS
            return flat[1][pl.ds(start, LOCAL, stride=FIELDS * HALO), :]
        return x_ref[pl.ds(field * ROWS + row, LOCAL, stride=FIELDS * ROWS), :]

    first, last = space == 0, space == SPACES - 1

    def outside(row):
        return first if row < 0 else last if row >= ROWS else None

    forecast = Forecast(load, outside)

    def block_copy(k):
        return pltpu.make_async_remote_copy(
            src_ref=sendbuf.at[k],
            dst_ref=values_ref.at[me],
            send_sem=a2a_send.at[k],
            recv_sem=a2a_recv.at[me],
            device_id=owner_id(k),
            device_id_type=MESH,
        )

    def emit(rows):
        for row in rows:
            for field in range(FIELDS):
                sendbuf[row, :, field * COLS : (field + 1) * COLS] = forecast.get(
                    field, STEPS, row
                )

    x_in.wait()
    emit(range(HALO, ROWS - HALO))
    pl.semaphore_wait(barrier, len(peers))

    up = pltpu.make_async_remote_copy(
        src_ref=x_halo_ref.at[:, 0],
        dst_ref=halo.at[1],
        send_sem=halo_send.at[0],
        recv_sem=halo_recv.at[1],
        device_id={"space": above},
        device_id_type=MESH,
    )
    down = pltpu.make_async_remote_copy(
        src_ref=x_halo_ref.at[:, ROWS // HALO - 1],
        dst_ref=halo.at[0],
        send_sem=halo_send.at[1],
        recv_sem=halo_recv.at[0],
        device_id={"space": below},
        device_id_type=MESH,
    )
    up.start()
    down.start()

    def is_inner(k):
        return jnp.logical_and(k >= HALO, k < ROWS - HALO)

    for k in owners:

        @pl.when(is_inner(k))
        def _():
            block_copy(k).start()

    up.wait()
    down.wait()
    emit(list(range(HALO)) + list(range(ROWS - HALO, ROWS)))
    for k in owners:

        @pl.when(jnp.logical_not(is_inner(k)))
        def _():
            block_copy(k).start()

    values_ref[me] = sendbuf[me]
    for k in owners:
        block_copy(k).wait_send()
    for k in owners:
        pltpu.make_async_remote_copy(
            src_ref=sendbuf.at[k],
            dst_ref=values_ref.at[k],
            send_sem=a2a_send.at[k],
            recv_sem=a2a_recv.at[k],
            device_id=owner_id(k),
            device_id_type=MESH,
        ).wait_recv()

    values = values_ref[...].reshape(ENSEMBLE, CELLS)
    mean = jnp.sum(values, axis=0, keepdims=True) * (1.0 / ENSEMBLE)
    scaled = (values - mean) * weight
    innovation = weight * (seen_value - mean)
    gram = dot_nt(scaled, scaled)
    pull = dot_nt(jnp.broadcast_to(innovation, (8, CELLS)), scaled)[0:1, :]
    left, right = gram[:, :COLS], gram[:, COLS:]
    mine[0] = left
    mine[1] = right
    mine[1, 0:1, :] = pull[:, :COLS]
    mine[1, 1:2, :] = pull[:, COLS:]

    def exchange(src, dst, sem_pair, slot_send, slot_recv, device):
        copy = pltpu.make_async_remote_copy(
            src_ref=src,
            dst_ref=dst,
            send_sem=sem_pair.at[0, slot_send],
            recv_sem=sem_pair.at[1, slot_recv],
            device_id=device,
            device_id_type=MESH,
        )
        copy.start()
        return copy

    partner = {"member": member + 1 - 2 * core}
    copy = exchange(mine.at[1 - core], corebuf, core_sem, 0, 0, partner)
    copy.wait()
    half = mine[core] + corebuf[...]
    x_to[...] = half.reshape(GROUPS, NY_CHIPS, 8, COLS)

    order = (4, 3, 5, 2, 6, 1, 7, 0)
    x_copies = {}
    for e in order:
        piece = lax.rem(y + e, NY_CHIPS)
        for d in range(1, GROUPS):
            there = lax.rem(group + d, GROUPS)
            sem_at = (d - 1) * NY_CHIPS + e
            src, dst = x_to.at[there, piece], x_from.at[d - 1, piece]
            x_copies[e, d] = exchange(src, dst, x_sem, sem_at, sem_at, {"group": there})
    copies = []
    for e in order:
        piece = lax.rem(y + e, NY_CHIPS)
        for d in range(1, GROUPS):
            x_copies[e, d].wait_recv()
        y_to[piece] = x_to[group, piece] + (
            x_from[0, piece] + x_from[1, piece] + x_from[2, piece]
        )
        if e > 0:
            src, dst = y_to.at[piece], y_from.at[e - 1]
            copies.append(exchange(src, dst, y_sem, e - 1, e - 1, y_peers[e - 1]))
    for copy in x_copies.values():
        copy.wait_send()
    for copy in copies:
        copy.wait()
    tile = y_to[y]
    for d in range(1, NY_CHIPS):
        tile = tile + y_from[d - 1]

    z_own[...] = tile
    z_from[z] = tile
    copies = []
    for d in range(1, NZ):
        copies.append(exchange(z_own, z_from.at[z], z_sem, d - 1, d - 1, z_peers[d - 1]))
    for copy in copies:
        copy.wait()
    total = z_from[0]
    for at in range(1, NZ):
        total = total + z_from[at]

    own = gram_ref.at[core, group]
    own[y] = total
    copies = []
    for d in range(1, NY_CHIPS):
        copies.append(exchange(own.at[y], own.at[y], gy_sem, d - 1, d - 1, y_peers[d - 1]))
    for copy in copies:
        copy.wait()

    copies = []
    for slot, (step, other) in enumerate(SETS):
        there = lax.rem(group + step, GROUPS)
        device = {"group": there, "member": member + other * (1 - 2 * core)}
        copies.append(exchange(own, own, gx_sem, slot, slot, device))
    for copy in copies:
        copy.wait()


STEPS = 2


def gather(state, values, precision, index):
    vmem = pl.BlockSpec(memory_space=pltpu.VMEM)
    hbm = pl.BlockSpec(memory_space=pltpu.HBM)
    dma = pltpu.SemaphoreType.DMA
    return pl.pallas_call(
        gather_kernel,
        out_shape=(
            jax.ShapeDtypeStruct((OWNERS, LOCAL, CELLS), F32),
            jax.ShapeDtypeStruct((2, GROUPS, NY_CHIPS, 8, COLS), F32),
        ),
        in_specs=[hbm, hbm, vmem, vmem, vmem],
        out_specs=(vmem, vmem),
        scratch_shapes=[
            pltpu.VMEM((LOCAL * FIELDS * ROWS, COLS), F32),
            pltpu.VMEM((2, LOCAL * FIELDS, HALO, COLS), F32),
            pltpu.VMEM((OWNERS, LOCAL, CELLS), F32),
            pltpu.VMEM((2, ENSEMBLE, COLS), F32),
            pltpu.VMEM((ENSEMBLE, COLS), F32),
            pltpu.VMEM((GROUPS - 1, NY_CHIPS, 8, COLS), F32),
            pltpu.VMEM((GROUPS, NY_CHIPS, 8, COLS), F32),
            pltpu.VMEM((NY_CHIPS - 1, 8, COLS), F32),
            pltpu.VMEM((NY_CHIPS, 8, COLS), F32),
            pltpu.VMEM((NZ, 8, COLS), F32),
            pltpu.VMEM((8, COLS), F32),
            dma,
            dma((2,)),
            dma((2,)),
            dma((OWNERS,)),
            dma((OWNERS,)),
            dma((2, 1)),
            dma((2, (GROUPS - 1) * NY_CHIPS)),
            dma((2, NY_CHIPS - 1)),
            dma((2, NZ - 1)),
            dma((2, NY_CHIPS - 1)),
            dma((2, len(SETS))),
        ],
        compiler_params=pltpu.CompilerParams(collective_id=0, has_side_effects=True),
        name="gather_and_gram",
    )(
        state.reshape(LOCAL * FIELDS * ROWS, COLS),
        state.reshape(LOCAL * FIELDS, ROWS // HALO, HALO, COLS),
        values,
        precision,
        index,
    )


def lane(tile, at):
    return jnp.broadcast_to(tile[:, at : at + 1], (SUB, COLS))

def sublane(tile, at):
    return jnp.broadcast_to(tile[at : at + 1, :], (SUB, COLS))

def total(terms):
    while len(terms) > 1:
        terms = [a + b for a, b in zip(terms[::2], terms[1::2])] + (
            [terms[-1]] if len(terms) % 2 else []
        )
    return terms[0]

def small_factor(columns):
    left = {(i, j): sublane(columns[j], i) for j in range(SUB) for i in range(j, SUB)}
    low, inv = {}, {}
    for j in range(0, SUB, 2):
        n = j + 1
        first, cross, second = left[j, j], left[n, j], left[n, n]
        root = lax.rsqrt(first)
        root_pair = lax.rsqrt(first * second - cross * cross)
        inv[j, j] = root
        inv[n, n] = root_pair * (first * root)
        for i in range(n, SUB):
            low[i, j] = left[i, j] * root
        for i in range(n + 1, SUB):
            low[i, n] = (left[i, n] - low[i, j] * low[n, j]) * inv[n, n]
        for k in range(n + 1, SUB):
            for i in range(k, SUB):
                left[i, k] = left[i, k] - low[i, j] * low[k, j] - low[i, n] * low[k, n]
    for j in range(SUB):
        for i in range(j + 1, SUB):
            terms = [low[i, k] * inv[k, j] for k in range(j, i)]
            inv[i, j] = -(total(terms) * inv[i, i])
    return inv

def invert_block(block, identity):
    wide = jnp.concatenate([block, identity], axis=1)
    tiles = [wide[SUB * q : SUB * (q + 1)] for q in range(BLOCK // SUB)]
    rows = lax.broadcasted_iota(jnp.int32, (SUB, COLS), 0)
    count = len(tiles)
    columns = [lane(tiles[0], j) for j in range(SUB)]
    for p in range(count):
        inv = small_factor(columns)
        terms = []
        for j in range(SUB):
            column = inv[SUB - 1, j]
            for i in range(SUB - 2, j - 1, -1):
                column = jnp.where(rows <= i, inv[i, j], column)
            if j > 0:
                column = jnp.where(rows < j, 0.0, column)
            terms.append(column * sublane(tiles[p], j))
        done = total(terms)
        spread = [sublane(done, k) for k in range(SUB)]
        for q in range(p + 1, count):
            source = [lane(tiles[q], SUB * p + j) for j in range(SUB)]
            low = [total([inv[k, j] * source[j] for j in range(k + 1)]) for k in range(SUB)]
            if q == p + 1:
                columns = [
                    lane(tiles[q], SUB * q + j)
                    - total([low[k] * sublane(low[k], j) for k in range(SUB)])
                    for j in range(SUB)
                ]
            tiles[q] = tiles[q] - total([low[k] * spread[k] for k in range(SUB)])
        tiles[p] = done
    return jnp.concatenate(tiles, axis=0)[:, BLOCK:]

def invert(work):
    n = ENSEMBLE // BLOCK
    r = lax.broadcasted_iota(jnp.int32, (BLOCK, BLOCK), 0)
    c = lax.broadcasted_iota(jnp.int32, (BLOCK, BLOCK), 1)
    identity = jnp.where(r == c, 1.0, 0.0)
    zero = jnp.zeros((BLOCK, BLOCK), F32)
    for k in range(n):
        at = k * BLOCK
        own = slice(at, at + BLOCK)
        rest = slice(at + BLOCK, ENSEMBLE)
        inverse = invert_block(work[own, own], identity)
        if k < n - 1:
            factor = dot_nt(work[rest, own], inverse)
        work[own, own] = identity
        solved = dot_nn(inverse, work[own, :])
        work[own, :] = solved
        if k < n - 1:
            work[rest, own] = jnp.zeros((ENSEMBLE - at - BLOCK, BLOCK), F32)
            work[rest, :] = work[rest, :] - dot_nn(factor, solved)

def make_transform(both_ref, work):
    r = lax.broadcasted_iota(jnp.int32, (COLS, COLS), 0)
    c = lax.broadcasted_iota(jnp.int32, (COLS, COLS), 1)
    eye = jnp.where(r == c, 1.0, 0.0)
    left = both_ref[0].reshape(ENSEMBLE, COLS)
    right = both_ref[1].reshape(ENSEMBLE, COLS)
    work[:COLS, :COLS] = left[:COLS] + eye
    work[COLS:, :COLS] = left[COLS:]
    work[:COLS, COLS:] = left[COLS:].T
    work[COLS:, COLS:] = right[COLS:] + eye
    pull = jnp.concatenate([right[0:1], right[1:2]], axis=1)
    invert(work)
    r = lax.broadcasted_iota(jnp.int32, (ENSEMBLE, ENSEMBLE), 0)
    c = lax.broadcasted_iota(jnp.int32, (ENSEMBLE, ENSEMBLE), 1)
    inverse = jnp.where(r >= c, work[...], 0.0)
    inner = dot_nt(jnp.broadcast_to(pull, (SUB, ENSEMBLE)), inverse)
    weights = dot_nn(inner, inverse)
    return inverse + weights[0:1, :]


def return_kernel(values_ref, both_ref, out_ref, work, sendbuf, arrived, send_sem, recv_sem):
    group, member, _ = place()
    me = group * MEMBERS + member
    barrier = pltpu.get_barrier_semaphore()
    owners = list(other_owners(group, member))
    for k in owners:
        pl.semaphore_signal(barrier, inc=1, device_id=owner_id(k), device_id_type=MESH)
    transform = make_transform(both_ref, work)
    work[...] = transform
    values = values_ref[...].reshape(ENSEMBLE, CELLS)
    mean = jnp.sum(values, axis=0, keepdims=True) * (1.0 / ENSEMBLE)
    anomaly = values - mean
    pl.semaphore_wait(barrier, OWNERS - 1)

    def copy(k, slot):
        return pltpu.make_async_remote_copy(
            src_ref=sendbuf.at[k],
            dst_ref=arrived.at[slot],
            send_sem=send_sem.at[k],
            recv_sem=recv_sem.at[slot],
            device_id=owner_id(k),
            device_id_type=MESH,
        )

    share = ENSEMBLE // GROUPS
    for step in (2, 1, 3, 0):
        there = lax.rem(group + step, GROUPS)
        part = dot_nn(work[pl.ds(pl.multiple_of(there * share, share), share), :], anomaly)
        sendbuf[pl.ds(there * MEMBERS, MEMBERS)] = (part + mean).reshape(
            MEMBERS, LOCAL, CELLS
        )
        for k, offset in zip(owners, OFFSETS):
            if offset[0] == step:
                copy(k, me).start()
    arrived[me] = sendbuf[me]
    for k in owners:
        copy(k, me).wait_send()
    for k in owners:
        copy(k, k).wait_recv()
    for row in range(ROWS):
        for field in range(FIELDS):
            out_ref[pl.ds(field * ROWS + row, LOCAL, stride=FIELDS * ROWS), :] = arrived[
                row, :, field * COLS : (field + 1) * COLS
            ]


def give_back(values, both):
    vmem = pl.BlockSpec(memory_space=pltpu.VMEM)
    dma = pltpu.SemaphoreType.DMA
    out = pl.pallas_call(
        return_kernel,
        out_shape=jax.ShapeDtypeStruct((LOCAL * FIELDS * ROWS, COLS), F32),
        in_specs=[vmem, vmem],
        out_specs=vmem,
        scratch_shapes=[
            pltpu.VMEM((ENSEMBLE, ENSEMBLE), F32),
            pltpu.VMEM((OWNERS, LOCAL, CELLS), F32),
            pltpu.VMEM((OWNERS, LOCAL, CELLS), F32),
            dma((OWNERS,)),
            dma((OWNERS,)),
        ],
        compiler_params=pltpu.CompilerParams(collective_id=1, has_side_effects=True),
        name="transform_and_return",
    )(values, both)
    return out.reshape(LOCAL, FIELDS, ROWS, COLS)


def on_device(height_velocity_tensor, obs_values, obs_precision, obs_index):
    values, both = gather(height_velocity_tensor, obs_values, obs_precision, obs_index)
    return give_back(values, both)


def solution(mesh):
    return jax.shard_map(
        on_device,
        mesh=mesh,
        in_specs=(
            P(("group", "member"), None, "space", None),
            P(("group", "member", "space"), None),
            P(("group", "member", "space"), None),
            P(("group", "member", "space"), None),
        ),
        out_specs=P(("group", "member"), None, "space", None),
        check_vma=False,
    )
```

```python
import math

import jax
import jax.numpy as jnp
from jax import lax
from jax.experimental import pallas as pl
from jax.experimental.pallas import tpu as pltpu
from jax.sharding import PartitionSpec as P

GRAV = 0.4
DEPTH = 0.4
GROUPS, MEMBERS, SPACES = 4, 8, 24
NZ, NY_CHIPS = 12, 8
OWNERS = GROUPS * MEMBERS
ROWS = 32
LOCAL = 8
ENSEMBLE = OWNERS * LOCAL
FIELDS = 3
COLS = 128
CELLS = FIELDS * COLS
OBS = 192
HALO = 4
BLOCK, SUB = 64, 8
MESH = pl.DeviceIdType.MESH
F32 = jnp.float32
HIGHEST = lax.Precision.HIGHEST
SCALE = 1.0 / math.sqrt(ENSEMBLE - 1)


def dot_nt(a, b):
    return lax.dot_general(
        a, b, (((1,), (1,)), ((), ())), precision=HIGHEST, preferred_element_type=F32
    )


def dot_nn(a, b):
    return lax.dot_general(
        a, b, (((1,), (0,)), ((), ())), precision=HIGHEST, preferred_element_type=F32
    )


def place():
    group = lax.axis_index("group")
    member = lax.axis_index("member")
    space = lax.axis_index("space")
    return group, member, space


def owner_id(k):
    return {"group": k // MEMBERS, "member": lax.rem(k, MEMBERS)}


SETS = [(2, 0), (2, 1), (1, 0), (1, 1), (3, 0), (3, 1), (0, 1)]


def hops(offset):
    return min(offset[0], GROUPS - offset[0]) + 3 * min(offset[1], 4 - offset[1])


OFFSETS = sorted(
    [(a, b, c) for a in range(GROUPS) for b in range(4) for c in range(2) if a + b + c],
    key=hops,
    reverse=True,
)


def other_owners(group, member):
    z_part, core = member // 2, lax.rem(member, 2)
    for a, b, c in OFFSETS:
        there = lax.rem(group + a, GROUPS) * MEMBERS
        yield there + lax.rem(z_part + b, 4) * 2 + lax.rem(core + c, 2)


def z_id(z, core, y):
    return {"member": z // 3 * 2 + core, "space": lax.rem(z, 3) * NY_CHIPS + y}


def across_y(field):
    return pltpu.roll(field, COLS - 1, 1) - pltpu.roll(field, 1, 1)


class Forecast:
    def __init__(self, load, outside):
        self.load = load
        self.outside = outside
        self.known = {}

    def masked(self, row, value):
        flag = self.outside(row)
        return value if flag is None else jnp.where(flag, 0.0, value)

    def get(self, field, step, row):
        key = (field, step, row)
        if key not in self.known:
            self.known[key] = self.compute(field, step, row)
        return self.known[key]

    def compute(self, field, step, row):
        if step == 0:
            return self.masked(row, self.load(field, row))
        if field == 1:
            ahead, behind = self.get(0, step - 1, row + 1), self.get(0, step - 1, row - 1)
            return self.masked(row, self.get(1, step - 1, row) - GRAV * (ahead - behind))
        if field == 2:
            return self.get(2, step - 1, row) - GRAV * across_y(self.get(0, step - 1, row))
        ahead, behind = self.get(1, step, row + 1), self.get(1, step, row - 1)
        change = ahead - behind + across_y(self.get(2, step, row))
        return self.masked(row, self.get(0, step - 1, row) - DEPTH * change)


def gather_kernel(
    x_hbm_ref,
    x_halo_ref,
    value_ref,
    precision_ref,
    index_ref,
    values_ref,
    gram_ref,
    x_ref,
    halo,
    sendbuf,
    mine,
    corebuf,
    x_from,
    x_to,
    y_from,
    y_to,
    z_from,
    z_own,
    x_in_sem,
    halo_send,
    halo_recv,
    a2a_send,
    a2a_recv,
    core_sem,
    x_sem,
    y_sem,
    z_sem,
    gy_sem,
    gx_sem,
):
    group, member, space = place()
    core = lax.rem(member, 2)
    z = member // 2 * 3 + space // NY_CHIPS
    y = lax.rem(space, NY_CHIPS)
    me = group * MEMBERS + member

    x_in = pltpu.make_async_copy(x_hbm_ref, x_ref, x_in_sem)
    x_in.start()

    barrier = pltpu.get_barrier_semaphore()
    above, below = lax.rem(space + SPACES - 1, SPACES), lax.rem(space + 1, SPACES)
    peers = [{"space": above}, {"space": below}]
    owners = list(other_owners(group, member))
    peers += [owner_id(k) for k in owners]
    y_peers = [
        {"space": space - y + lax.rem(y + d, NY_CHIPS)} for d in range(1, NY_CHIPS)
    ]
    z_peers = [z_id(lax.rem(z + d, NZ), core, y) for d in range(1, NZ)]
    peers += y_peers + z_peers
    for peer in peers:
        pl.semaphore_signal(barrier, inc=1, device_id=peer, device_id_type=MESH)

    cells = lax.broadcasted_iota(jnp.int32, (CELLS, OBS), 0)
    picked = jnp.where(cells == index_ref[0:1, :], 1.0, 0.0)
    spread = dot_nt(jnp.broadcast_to(precision_ref[...], (SUB, OBS)), picked)
    weight = spread[0:1, :] * SCALE
    spread = dot_nt(jnp.broadcast_to(value_ref[...], (SUB, OBS)), picked)
    seen_value = spread[0:1, :]

    flat = [halo.at[i].reshape(LOCAL * FIELDS * HALO, COLS) for i in range(2)]

    def load(field, row):
        if row < 0:
            start = field * HALO + row + HALO
            return flat[0][pl.ds(start, LOCAL, stride=FIELDS * HALO), :]
        if row >= ROWS:
            start = field * HALO + row - ROWS
            return flat[1][pl.ds(start, LOCAL, stride=FIELDS * HALO), :]
        return x_ref[pl.ds(field * ROWS + row, LOCAL, stride=FIELDS * ROWS), :]

    first, last = space == 0, space == SPACES - 1

    def outside(row):
        return first if row < 0 else last if row >= ROWS else None

    forecast = Forecast(load, outside)

    def block_copy(k):
        return pltpu.make_async_remote_copy(
            src_ref=sendbuf.at[k],
            dst_ref=values_ref.at[me],
            send_sem=a2a_send.at[k],
            recv_sem=a2a_recv.at[me],
            device_id=owner_id(k),
            device_id_type=MESH,
        )

    def emit(rows):
        for row in rows:
            for field in range(FIELDS):
                sendbuf[row, :, field * COLS : (field + 1) * COLS] = forecast.get(
                    field, STEPS, row
                )

    x_in.wait()
    emit(range(HALO, ROWS - HALO))
    pl.semaphore_wait(barrier, len(peers))

    up = pltpu.make_async_remote_copy(
        src_ref=x_halo_ref.at[:, 0],
        dst_ref=halo.at[1],
        send_sem=halo_send.at[0],
        recv_sem=halo_recv.at[1],
        device_id={"space": above},
        device_id_type=MESH,
    )
    down = pltpu.make_async_remote_copy(
        src_ref=x_halo_ref.at[:, ROWS // HALO - 1],
        dst_ref=halo.at[0],
        send_sem=halo_send.at[1],
        recv_sem=halo_recv.at[0],
        device_id={"space": below},
        device_id_type=MESH,
    )
    up.start()
    down.start()

    def is_inner(k):
        return jnp.logical_and(k >= HALO, k < ROWS - HALO)

    for k in owners:

        @pl.when(is_inner(k))
        def _():
            block_copy(k).start()

    up.wait()
    down.wait()
    emit(list(range(HALO)) + list(range(ROWS - HALO, ROWS)))
    for k in owners:

        @pl.when(jnp.logical_not(is_inner(k)))
        def _():
            block_copy(k).start()

    values_ref[me] = sendbuf[me]
    for k in owners:
        block_copy(k).wait_send()
    for k in owners:
        pltpu.make_async_remote_copy(
            src_ref=sendbuf.at[k],
            dst_ref=values_ref.at[k],
            send_sem=a2a_send.at[k],
            recv_sem=a2a_recv.at[k],
            device_id=owner_id(k),
            device_id_type=MESH,
        ).wait_recv()

    values = values_ref[...].reshape(ENSEMBLE, CELLS)
    mean = jnp.sum(values, axis=0, keepdims=True) * (1.0 / ENSEMBLE)
    scaled = (values - mean) * weight
    innovation = weight * (seen_value - mean)
    gram = dot_nt(scaled, scaled)
    pull = dot_nt(jnp.broadcast_to(innovation, (8, CELLS)), scaled)[0:1, :]
    left, right = gram[:, :COLS], gram[:, COLS:]
    mine[0] = left
    mine[1] = right
    mine[1, 0:1, :] = pull[:, :COLS]
    mine[1, 1:2, :] = pull[:, COLS:]

    def exchange(src, dst, sem_pair, slot_send, slot_recv, device):
        copy = pltpu.make_async_remote_copy(
            src_ref=src,
            dst_ref=dst,
            send_sem=sem_pair.at[0, slot_send],
            recv_sem=sem_pair.at[1, slot_recv],
            device_id=device,
            device_id_type=MESH,
        )
        copy.start()
        return copy

    partner = {"member": member + 1 - 2 * core}
    copy = exchange(mine.at[1 - core], corebuf, core_sem, 0, 0, partner)
    copy.wait()
    half = mine[core] + corebuf[...]
    x_to[...] = half.reshape(GROUPS, NY_CHIPS, 8, COLS)

    order = (4, 3, 5, 2, 6, 1, 7, 0)
    x_copies = {}
    for e in order:
        piece = lax.rem(y + e, NY_CHIPS)
        for d in range(1, GROUPS):
            there = lax.rem(group + d, GROUPS)
            sem_at = (d - 1) * NY_CHIPS + e
            src, dst = x_to.at[there, piece], x_from.at[d - 1, piece]
            x_copies[e, d] = exchange(src, dst, x_sem, sem_at, sem_at, {"group": there})
    copies = []
    for e in order:
        piece = lax.rem(y + e, NY_CHIPS)
        for d in range(1, GROUPS):
            x_copies[e, d].wait_recv()
        y_to[piece] = x_to[group, piece] + (
            x_from[0, piece] + x_from[1, piece] + x_from[2, piece]
        )
        if e > 0:
            src, dst = y_to.at[piece], y_from.at[e - 1]
            copies.append(exchange(src, dst, y_sem, e - 1, e - 1, y_peers[e - 1]))
    for copy in x_copies.values():
        copy.wait_send()
    for copy in copies:
        copy.wait()
    tile = y_to[y]
    for d in range(1, NY_CHIPS):
        tile = tile + y_from[d - 1]

    z_own[...] = tile
    z_from[z] = tile
    copies = []
    for d in (6, 5, 7, 4, 8, 3, 9, 2, 10, 1, 11):
        copies.append(exchange(z_own, z_from.at[z], z_sem, d - 1, d - 1, z_peers[d - 1]))
    for copy in copies:
        copy.wait()
    total = z_from[0]
    for at in range(1, NZ):
        total = total + z_from[at]

    own = gram_ref.at[core, group]
    own[y] = total
    copies = []
    for d in (4, 3, 5, 2, 6, 1, 7):
        copies.append(exchange(own.at[y], own.at[y], gy_sem, d - 1, d - 1, y_peers[d - 1]))
    for copy in copies:
        copy.wait()

    copies = []
    for slot, (step, other) in enumerate(SETS):
        there = lax.rem(group + step, GROUPS)
        device = {"group": there, "member": member + other * (1 - 2 * core)}
        copies.append(exchange(own, own, gx_sem, slot, slot, device))
    for copy in copies:
        copy.wait()


STEPS = 2


def gather(state, values, precision, index):
    vmem = pl.BlockSpec(memory_space=pltpu.VMEM)
    hbm = pl.BlockSpec(memory_space=pltpu.HBM)
    dma = pltpu.SemaphoreType.DMA
    return pl.pallas_call(
        gather_kernel,
        out_shape=(
            jax.ShapeDtypeStruct((OWNERS, LOCAL, CELLS), F32),
            jax.ShapeDtypeStruct((2, GROUPS, NY_CHIPS, 8, COLS), F32),
        ),
        in_specs=[hbm, hbm, vmem, vmem, vmem],
        out_specs=(vmem, vmem),
        scratch_shapes=[
            pltpu.VMEM((LOCAL * FIELDS * ROWS, COLS), F32),
            pltpu.VMEM((2, LOCAL * FIELDS, HALO, COLS), F32),
            pltpu.VMEM((OWNERS, LOCAL, CELLS), F32),
            pltpu.VMEM((2, ENSEMBLE, COLS), F32),
            pltpu.VMEM((ENSEMBLE, COLS), F32),
            pltpu.VMEM((GROUPS - 1, NY_CHIPS, 8, COLS), F32),
            pltpu.VMEM((GROUPS, NY_CHIPS, 8, COLS), F32),
            pltpu.VMEM((NY_CHIPS - 1, 8, COLS), F32),
            pltpu.VMEM((NY_CHIPS, 8, COLS), F32),
            pltpu.VMEM((NZ, 8, COLS), F32),
            pltpu.VMEM((8, COLS), F32),
            dma,
            dma((2,)),
            dma((2,)),
            dma((OWNERS,)),
            dma((OWNERS,)),
            dma((2, 1)),
            dma((2, (GROUPS - 1) * NY_CHIPS)),
            dma((2, NY_CHIPS - 1)),
            dma((2, NZ - 1)),
            dma((2, NY_CHIPS - 1)),
            dma((2, len(SETS))),
        ],
        compiler_params=pltpu.CompilerParams(collective_id=0, has_side_effects=True),
        name="gather_and_gram",
    )(
        state.reshape(LOCAL * FIELDS * ROWS, COLS),
        state.reshape(LOCAL * FIELDS, ROWS // HALO, HALO, COLS),
        values,
        precision,
        index,
    )


def lane(tile, at):
    return jnp.broadcast_to(tile[:, at : at + 1], (SUB, COLS))

def sublane(tile, at):
    return jnp.broadcast_to(tile[at : at + 1, :], (SUB, COLS))

def total(terms):
    while len(terms) > 1:
        terms = [a + b for a, b in zip(terms[::2], terms[1::2])] + (
            [terms[-1]] if len(terms) % 2 else []
        )
    return terms[0]

def small_factor(columns):
    left = {(i, j): sublane(columns[j], i) for j in range(SUB) for i in range(j, SUB)}
    low, inv = {}, {}
    for j in range(0, SUB, 2):
        n = j + 1
        first, cross, second = left[j, j], left[n, j], left[n, n]
        root = lax.rsqrt(first)
        root_pair = lax.rsqrt(first * second - cross * cross)
        inv[j, j] = root
        inv[n, n] = root_pair * (first * root)
        for i in range(n, SUB):
            low[i, j] = left[i, j] * root
        for i in range(n + 1, SUB):
            low[i, n] = (left[i, n] - low[i, j] * low[n, j]) * inv[n, n]
        for k in range(n + 1, SUB):
            for i in range(k, SUB):
                left[i, k] = left[i, k] - low[i, j] * low[k, j] - low[i, n] * low[k, n]
    for j in range(SUB):
        for i in range(j + 1, SUB):
            terms = [low[i, k] * inv[k, j] for k in range(j, i)]
            inv[i, j] = -(total(terms) * inv[i, i])
    return inv

def invert_block(block, identity):
    wide = jnp.concatenate([block, identity], axis=1)
    tiles = [wide[SUB * q : SUB * (q + 1)] for q in range(BLOCK // SUB)]
    rows = lax.broadcasted_iota(jnp.int32, (SUB, COLS), 0)
    count = len(tiles)
    columns = [lane(tiles[0], j) for j in range(SUB)]
    for p in range(count):
        inv = small_factor(columns)
        terms = []
        for j in range(SUB):
            column = inv[SUB - 1, j]
            for i in range(SUB - 2, j - 1, -1):
                column = jnp.where(rows <= i, inv[i, j], column)
            if j > 0:
                column = jnp.where(rows < j, 0.0, column)
            terms.append(column * sublane(tiles[p], j))
        done = total(terms)
        spread = [sublane(done, k) for k in range(SUB)]
        for q in range(p + 1, count):
            source = [lane(tiles[q], SUB * p + j) for j in range(SUB)]
            low = [total([inv[k, j] * source[j] for j in range(k + 1)]) for k in range(SUB)]
            if q == p + 1:
                columns = [
                    lane(tiles[q], SUB * q + j)
                    - total([low[k] * sublane(low[k], j) for k in range(SUB)])
                    for j in range(SUB)
                ]
            tiles[q] = tiles[q] - total([low[k] * spread[k] for k in range(SUB)])
        tiles[p] = done
    return jnp.concatenate(tiles, axis=0)[:, BLOCK:]

def invert(work):
    n = ENSEMBLE // BLOCK
    r = lax.broadcasted_iota(jnp.int32, (BLOCK, BLOCK), 0)
    c = lax.broadcasted_iota(jnp.int32, (BLOCK, BLOCK), 1)
    identity = jnp.where(r == c, 1.0, 0.0)
    zero = jnp.zeros((BLOCK, BLOCK), F32)
    diagonal = work[:BLOCK, :BLOCK]
    for k in range(n):
        at = k * BLOCK
        own = slice(at, at + BLOCK)
        rest = slice(at + BLOCK, ENSEMBLE)
        following = slice(at + BLOCK, at + 2 * BLOCK)
        inverse = invert_block(diagonal, identity)
        if k < n - 1:
            near = dot_nt(work[following, own], inverse)
            diagonal = work[following, following] - dot_nt(near, near)
            factor = dot_nt(work[rest, own], inverse)
        work[own, own] = identity
        solved = dot_nn(inverse, work[own, :])
        work[own, :] = solved
        if k < n - 1:
            work[rest, own] = jnp.zeros((ENSEMBLE - at - BLOCK, BLOCK), F32)
            work[rest, :] = work[rest, :] - dot_nn(factor, solved)


def make_transform(both_ref, work):
    r = lax.broadcasted_iota(jnp.int32, (COLS, COLS), 0)
    c = lax.broadcasted_iota(jnp.int32, (COLS, COLS), 1)
    eye = jnp.where(r == c, 1.0, 0.0)
    left = both_ref[0].reshape(ENSEMBLE, COLS)
    right = both_ref[1].reshape(ENSEMBLE, COLS)
    work[:COLS, :COLS] = left[:COLS] + eye
    work[COLS:, :COLS] = left[COLS:]
    work[:COLS, COLS:] = left[COLS:].T
    work[COLS:, COLS:] = right[COLS:] + eye
    pull = jnp.concatenate([right[0:1], right[1:2]], axis=1)
    invert(work)
    r = lax.broadcasted_iota(jnp.int32, (ENSEMBLE, ENSEMBLE), 0)
    c = lax.broadcasted_iota(jnp.int32, (ENSEMBLE, ENSEMBLE), 1)
    inverse = jnp.where(r >= c, work[...], 0.0)
    inner = dot_nt(jnp.broadcast_to(pull, (SUB, ENSEMBLE)), inverse)
    weights = dot_nn(inner, inverse)
    return inverse + weights[0:1, :]


def return_kernel(values_ref, both_ref, out_ref, work, sendbuf, arrived, send_sem, recv_sem):
    group, member, _ = place()
    me = group * MEMBERS + member
    barrier = pltpu.get_barrier_semaphore()
    owners = list(other_owners(group, member))
    for k in owners:
        pl.semaphore_signal(barrier, inc=1, device_id=owner_id(k), device_id_type=MESH)
    transform = make_transform(both_ref, work)
    work[...] = transform
    values = values_ref[...].reshape(ENSEMBLE, CELLS)
    mean = jnp.sum(values, axis=0, keepdims=True) * (1.0 / ENSEMBLE)
    anomaly = values - mean
    pl.semaphore_wait(barrier, OWNERS - 1)

    def copy(k, slot):
        return pltpu.make_async_remote_copy(
            src_ref=sendbuf.at[k],
            dst_ref=arrived.at[slot],
            send_sem=send_sem.at[k],
            recv_sem=recv_sem.at[slot],
            device_id=owner_id(k),
            device_id_type=MESH,
        )

    share = ENSEMBLE // GROUPS
    for step in (2, 1, 3, 0):
        there = lax.rem(group + step, GROUPS)
        part = dot_nn(work[pl.ds(pl.multiple_of(there * share, share), share), :], anomaly)
        sendbuf[pl.ds(there * MEMBERS, MEMBERS)] = (part + mean).reshape(
            MEMBERS, LOCAL, CELLS
        )
        for k, offset in zip(owners, OFFSETS):
            if offset[0] == step:
                copy(k, me).start()
    arrived[me] = sendbuf[me]
    for k in owners:
        copy(k, me).wait_send()
    for k in owners:
        copy(k, k).wait_recv()
    for row in range(ROWS):
        for field in range(FIELDS):
            out_ref[pl.ds(field * ROWS + row, LOCAL, stride=FIELDS * ROWS), :] = arrived[
                row, :, field * COLS : (field + 1) * COLS
            ]


def give_back(values, both):
    vmem = pl.BlockSpec(memory_space=pltpu.VMEM)
    dma = pltpu.SemaphoreType.DMA
    out = pl.pallas_call(
        return_kernel,
        out_shape=jax.ShapeDtypeStruct((LOCAL * FIELDS * ROWS, COLS), F32),
        in_specs=[vmem, vmem],
        out_specs=vmem,
        scratch_shapes=[
            pltpu.VMEM((ENSEMBLE, ENSEMBLE), F32),
            pltpu.VMEM((OWNERS, LOCAL, CELLS), F32),
            pltpu.VMEM((OWNERS, LOCAL, CELLS), F32),
            dma((OWNERS,)),
            dma((OWNERS,)),
        ],
        compiler_params=pltpu.CompilerParams(collective_id=1, has_side_effects=True),
        name="transform_and_return",
    )(values, both)
    return out.reshape(LOCAL, FIELDS, ROWS, COLS)


def on_device(height_velocity_tensor, obs_values, obs_precision, obs_index):
    values, both = gather(height_velocity_tensor, obs_values, obs_precision, obs_index)
    return give_back(values, both)


def solution(mesh):
    return jax.shard_map(
        on_device,
        mesh=mesh,
        in_specs=(
            P(("group", "member"), None, "space", None),
            P(("group", "member", "space"), None),
            P(("group", "member", "space"), None),
            P(("group", "member", "space"), None),
        ),
        out_specs=P(("group", "member"), None, "space", None),
        check_vma=False,
    )
```
